32 devices in a mesh: img: 8 (over y, x, core), feat: 4 (over z).
Axes of the slice: x: 2, y: 2, z: 4, core: 2. Of those that a mesh axis runs over, the one named last changes fastest.
Arguments:
- coeffs: bfloat16 [16384, 512], P('img', 'feat'), may hold values from -16 to 16
- triples: int32 [3, 16384], P(None, 'feat'), may hold values from 0 to 510, as said below
- sketch: int32 [16384, 128], P('feat'), may hold values from -1 to 1
Outputs:
- basis: float32 [16384, 128], P('img')
- projected: float32 [128, 16384], P('img', 'feat')
The draws below stay inside these ranges and needn't reach their ends.
Inputs may be any that keep to these rules, and one draw needn't show every extreme that they name: `triples`: every column is a triple k1, k2, k1 + k2 with k1 and k2 below 256.
All inputs are finite; a program needn't handle non-finite values.
Results may differ from the reference program's by a relative error of at most 0.0044.
Values may be sent and summed in bfloat16 or wider, within the bound.
A program may use at most 192 MiB of HBM per device.

```python
import math
import jax
import jax.numpy as jnp
from jax import lax

COEFS = 512
RANK = 128
IMAGES = 16384
FEATS = 16384


def draw_coeffs(key, part):
    noise_key = jax.random.fold_in(key, 11)
    scale_key = jax.random.fold_in(key, 12)
    row_draw = jax.random.uniform(scale_key, (IMAGES, 1), jnp.float32)
    ramp = jnp.arange(IMAGES, dtype=jnp.float32)[:, None] / IMAGES
    values = jax.random.normal(noise_key, (IMAGES, COEFS), jnp.float32)
    spread = math.log(10.0)
    row_scale = jnp.exp((spread * row_draw + math.log(3.0) * ramp) / 3.0)
    return jnp.clip(values * row_scale, -16.0, 16.0).astype(jnp.bfloat16)


def draw_triples(key, part):
    first_key = jax.random.fold_in(key, 21)
    second_key = jax.random.fold_in(key, 22)
    first_index = jax.random.randint(first_key, (FEATS,), 0, COEFS // 2, dtype=jnp.int32)
    second_index = jax.random.randint(second_key, (FEATS,), 0, COEFS // 2, dtype=jnp.int32)
    return jnp.stack([first_index, second_index, first_index + second_index]).astype(jnp.int32)


def place_ends(drawn, rng, smallest, high):
    dims = drawn.shape
    place = [jax.random.randint(jax.random.fold_in(rng, axis), (), 0, dims[axis]) for axis in range(len(dims))]
    drawn = drawn.at[tuple(place)].set(smallest)
    longest = dims.index(max(dims))
    place[longest] = (place[longest] + 1) % dims[longest]
    return drawn.at[tuple(place)].set(high)


def setup_inputs(seed: int = 0) -> dict:
    key_of = jax.random.split(jax.random.key(seed), 4)
    return {
        "coeffs": draw_coeffs(jax.random.fold_in(key_of[3], 71), 0),
        "triples": draw_triples(jax.random.fold_in(key_of[3], 71), 0),
        "sketch": place_ends(jax.random.randint(key_of[2], (FEATS, RANK), -1, 2), jax.random.fold_in(key_of[2], 1), -1, 1).astype(jnp.int32),
    }


def features_block(coeffs, triples, first_col, block_width):
    chosen_cols = lax.dynamic_slice_in_dim(triples, first_col, block_width, 1)
    widened = coeffs.astype(jnp.float32)
    product = jnp.take(widened, chosen_cols[0], axis=1) * jnp.take(widened, chosen_cols[1], axis=1)
    product = product * jnp.take(widened, chosen_cols[2], axis=1)
    return product.astype(jnp.bfloat16)

def reference(coeffs, triples, sketch):
    total_rows = coeffs.shape[0]
    total_feats = triples.shape[1]
    block_width = min(4096, total_feats)
    block_count = total_feats // block_width
    sketch_scale = (1.5 / total_feats) ** 0.5

    def sketch_step(carry, block_index):
        first_col = (block_index * block_width).astype(jnp.int32)
        feature_tile = features_block(coeffs, triples, first_col, block_width)
        signs = lax.dynamic_slice_in_dim(sketch, first_col, block_width, 0).astype(jnp.bfloat16)
        return (carry + jnp.dot(feature_tile.astype(jnp.float32), signs.astype(jnp.float32), preferred_element_type=jnp.float32), None)
    summed, unused = lax.scan(sketch_step, jnp.zeros((total_rows, RANK), jnp.float32), jnp.arange(block_count, dtype=jnp.int32))
    sketched = summed * sketch_scale
    gram = jnp.dot(sketched.T, sketched, precision=lax.Precision.HIGHEST) / total_rows
    lower = jnp.linalg.cholesky(gram)
    basis = lax.linalg.triangular_solve(lower, sketched.T, left_side=True, lower=True).T

    def project(block_index):
        first_col = (block_index * block_width).astype(jnp.int32)
        feature_tile = features_block(coeffs, triples, first_col, block_width)
        return jnp.dot(basis.T, feature_tile.astype(jnp.float32), precision=lax.Precision.HIGHEST)
    blocks = lax.map(project, jnp.arange(block_count, dtype=jnp.int32))
    projected = jnp.transpose(blocks, (1, 0, 2)).reshape(RANK, total_feats) / jnp.sqrt(jnp.float32(total_rows))
    return (basis, projected)
```

```python
import functools

import jax
import jax.numpy as jnp
from jax import lax
from jax.experimental import pallas as pl
from jax.experimental.pallas import tpu as pltpu
from jax.sharding import PartitionSpec as P

CHUNKS = 8
MESH = pl.DeviceIdType.MESH
VMEM = pl.BlockSpec(memory_space=pltpu.VMEM)


def greet(axis, peers):
    barrier = pltpu.get_barrier_semaphore()
    for peer in peers:
        pl.semaphore_signal(barrier, inc=1, device_id={axis: peer}, device_id_type=MESH)
    pl.semaphore_wait(barrier, len(peers))


def gather_kernel(
    count, width, coeffs_ref, triples_ref, sketch_ref, tile_ref, value_ref, blocks, sel_ref, signs_ref,
    sum_ref, part_ref, slots, full_ref, own_sem, send_sem, recv_sem, to_sem, from_sem, out_sem, in_sem
):
    me = lax.axis_index("feat")
    rows, part = coeffs_ref.shape
    step = rows // CHUNKS
    half = count * part // 2
    tiles = sketch_ref.shape[0] // width
    spans = ((0, half), (half, half), (2 * half, 2 * half))

    def build(index):
        start, depth = spans[index]

        def one(j, carry):
            cols = pl.ds(pl.multiple_of(j * width, width), width)
            levels = lax.broadcasted_iota(jnp.int32, (depth, width), 0)
            chosen = triples_ref[index : index + 1, cols]
            sel_ref[start : start + depth, cols] = jnp.where(levels == chosen, 1.0, 0.0).astype(jnp.bfloat16)
            if index == 0:
                signs_ref[cols, :] = sketch_ref[cols, :].astype(jnp.float32).astype(jnp.bfloat16)
            return carry

        lax.fori_loop(0, tiles, one, 0)

    own = pltpu.make_async_copy(coeffs_ref, blocks.at[me], own_sem)
    own.start()
    peers = peers_of(me, count)
    piece = step // count
    greet("feat", peers)
    own.wait()

    def copy(side, hop, chunk, source, target):
        span = blocks.at[source, pl.ds(pl.multiple_of(chunk * step, step), step)]
        return pltpu.make_async_remote_copy(
            src_ref=span,
            dst_ref=span,
            send_sem=send_sem.at[side, hop, chunk],
            recv_sem=recv_sem.at[side, hop, chunk],
            device_id={"feat": target},
            device_id_type=MESH,
        )

    def rows_of(chunk, owner):
        return pl.ds(pl.multiple_of(chunk * step + owner * piece, piece), piece)

    def reduce_copy(k, chunk):
        return pltpu.make_async_remote_copy(
            src_ref=part_ref.at[rows_of(chunk, peers[k])],
            dst_ref=slots.at[k, chunk],
            send_sem=to_sem.at[k, chunk],
            recv_sem=from_sem.at[k, chunk],
            device_id={"feat": peers[k]},
            device_id_type=MESH,
        )

    def spread_copy(k, chunk, owner):
        span = full_ref.at[rows_of(chunk, owner)]
        return pltpu.make_async_remote_copy(
            src_ref=span,
            dst_ref=span,
            send_sem=out_sem.at[k, chunk],
            recv_sem=in_sem.at[k, chunk],
            device_id={"feat": peers[k]},
            device_id_type=MESH,
        )

    def one_round(turn, carry):
        for hop in range(count):
            chunk = turn - hop
            live = (chunk >= 0) & (chunk < CHUNKS)
            if hop > 0:

                @pl.when(live & (me >= hop))
                def _():
                    copy(0, hop - 1, chunk, me - hop, me - 1).wait_recv()

                @pl.when(live & (me + hop < count))
                def _():
                    copy(1, hop - 1, chunk, me + hop, me + 1).wait_recv()

            if hop < count - 1:

                @pl.when(live & (me >= hop) & (me < count - 1))
                def _():
                    copy(0, hop, chunk, me - hop, me + 1).start()

                @pl.when(live & (me + hop < count) & (me > 0))
                def _():
                    copy(1, hop, chunk, me + hop, me - 1).start()

        for index in range(3):

            @pl.when(turn == min(index, count - 2))
            def _():
                build(index)

        base = turn - (count - 1)

        @pl.when((base >= 1) & (base <= CHUNKS))
        def _():
            for k in range(count - 1):
                reduce_copy(k, base - 1).start()

        @pl.when(base >= 2)
        def _():
            for k in range(count - 1):
                spread_copy(k, base - 2, me).start()

        @pl.when((base >= 0) & (base < CHUNKS))
        def _():
            first_row = pl.multiple_of(base * step, step)
            here = pl.ds(first_row, step)
            sum_ref[...] = jnp.zeros(sum_ref.shape, jnp.float32)
            low = jnp.concatenate([blocks[s, here, :] for s in range(count // 2)], axis=1)
            high = jnp.concatenate([blocks[s, here, :] for s in range(count // 2, count)], axis=1)
            full = jnp.concatenate([low, high], axis=1)

            def one_tile(j, unused):
                cols = pl.ds(pl.multiple_of(j * width, width), width)
                first = jnp.dot(low, sel_ref[:half, cols], preferred_element_type=jnp.float32)
                second = jnp.dot(low, sel_ref[half : 2 * half, cols], preferred_element_type=jnp.float32)
                third = jnp.dot(full, sel_ref[2 * half :, cols], preferred_element_type=jnp.float32)
                tile = (first * second * third).astype(jnp.bfloat16)
                tile_ref[here, cols] = tile
                sum_ref[...] += jnp.dot(tile, signs_ref[cols, :], preferred_element_type=jnp.float32)
                return unused

            lax.fori_loop(0, tiles, one_tile, 0, unroll=2)
            part_ref[here, :] = sum_ref[...].astype(jnp.bfloat16)

        @pl.when((base >= 1) & (base <= CHUNKS))
        def _():
            mine = rows_of(base - 1, me)
            total = part_ref[mine, :].astype(jnp.float32)
            for k in range(count - 1):
                reduce_copy(k, base - 1).wait_recv()
                total = total + slots[k, base - 1].astype(jnp.float32)
            full_ref[mine, :] = total.astype(jnp.bfloat16)

        return carry

    lax.fori_loop(0, CHUNKS + count + 1, one_round, 0)

    def drain(chunk, carry):
        for k in range(count - 1):
            spread_copy(k, chunk, lax.rem(me + count - 1 - k, count)).wait_recv()
            spread_copy(k, chunk, me).wait_send()
            reduce_copy(k, chunk).wait_send()
        for hop in range(count - 1):

            @pl.when((me >= hop) & (me < count - 1))
            def _():
                copy(0, hop, chunk, me - hop, me + 1).wait_send()

            @pl.when((me + hop < count) & (me > 0))
            def _():
                copy(1, hop, chunk, me + hop, me - 1).wait_send()

        return carry

    lax.fori_loop(0, CHUNKS, drain, 0)
    value_ref[...] = full_ref[...]


def gather_features(coeffs, triples, sketch, count):
    rows, part = coeffs.shape
    feats, rank = sketch.shape
    hops = max(count - 1, 1)
    step = rows // CHUNKS
    return pl.pallas_call(
        functools.partial(gather_kernel, count, min(512, feats)),
        in_specs=[VMEM] * 3,
        out_specs=[VMEM] * 2,
        out_shape=[
            jax.ShapeDtypeStruct((rows, feats), jnp.bfloat16),
            jax.ShapeDtypeStruct((rows, rank), jnp.bfloat16),
        ],
        scratch_shapes=[
            pltpu.VMEM((count, rows, part), jnp.bfloat16),
            pltpu.VMEM((2 * count * part, feats), jnp.bfloat16),
            pltpu.VMEM((feats, rank), jnp.bfloat16),
            pltpu.VMEM((step, rank), jnp.float32),
            pltpu.VMEM((rows, rank), jnp.bfloat16),
            pltpu.VMEM((hops, CHUNKS, step // count, rank), jnp.bfloat16),
            pltpu.VMEM((rows, rank), jnp.bfloat16),
            pltpu.SemaphoreType.DMA,
            pltpu.SemaphoreType.DMA((2, hops, CHUNKS)),
            pltpu.SemaphoreType.DMA((2, hops, CHUNKS)),
        ]
        + [pltpu.SemaphoreType.DMA((hops, CHUNKS))] * 4,
        compiler_params=pltpu.CompilerParams(
            collective_id=0, has_side_effects=True, vmem_limit_bytes=24 << 20
        ),
    )(coeffs, triples, sketch)


def peers_of(me, count):
    return [lax.rem(me + k, count) for k in range(1, count)]


def factor_panels(scale, after, gram, left, right, pivots, out_ref, width):
    size = gram.shape[0]
    rows = lax.broadcasted_iota(jnp.int32, (width, size), 0)
    lanes = lax.broadcasted_iota(jnp.int32, (width, size), 1)
    left[...] = gram * scale
    whole_rows = lax.broadcasted_iota(jnp.int32, (size, size), 0)
    whole_lanes = lax.broadcasted_iota(jnp.int32, (size, size), 1)
    right[...] = jnp.where(whole_rows == whole_lanes, 1.0, 0.0)

    def panel(p, carry):
        first = pl.multiple_of(p * width, width)
        here = pl.ds(first, width)
        block = left[here, :]
        twin = right[here, :]
        inverse = jnp.zeros((width, size), jnp.float32)
        kept = jnp.zeros((width, size), jnp.float32)
        for j in range(width):
            column = jnp.take_along_axis(block, jnp.full((width, size), first + j, jnp.int32), axis=1)
            pivot = column[j : j + 1, :]
            ratio = 1.0 / pivot
            inverse = jnp.where(rows == j, ratio, inverse)
            kept = jnp.where(rows == j, pivot, kept)
            if j + 1 < width:
                factor = jnp.where(rows > j, column * ratio, 0.0)
                block = block - factor * block[j : j + 1, :]
                twin = twin - factor * twin[j : j + 1, :]
        pivots[here, :] = kept
        right[here, :] = twin

        @pl.when(p + 1 < size // width)
        def _():
            factor = jnp.where(lanes >= first + width, block * inverse, 0.0)
            across = (((0,), (0,)), ((), ()))
            exact = lax.Precision.HIGHEST
            left[...] -= lax.dot_general(factor, block, across, precision=exact, preferred_element_type=jnp.float32)
            right[...] -= lax.dot_general(factor, twin, across, precision=exact, preferred_element_type=jnp.float32)

        return carry

    lax.fori_loop(0, size // width, panel, 0)
    out_ref[...] = right[...] * (after / jnp.sqrt(pivots[...]))


def finish_kernel(
    count, scale, after, root, value_ref, tile_ref, inverse_ref, out_ref, turned, gram_slots, staged, raw_slots,
    solved_ref, row_slots, left, right, pivots, gram_send, gram_recv, raw_send, raw_recv, row_send, row_recv
):
    me = lax.axis_index("img")
    peers = peers_of(me, count)
    others = count - 1
    span = tile_ref.shape[1] // count
    part = out_ref.shape[0]

    def columns(owner):
        return pl.ds(pl.multiple_of(owner * span, span), span)

    def remote(source, target, send, recv, k):
        return pltpu.make_async_remote_copy(
            src_ref=source,
            dst_ref=target,
            send_sem=send.at[k],
            recv_sem=recv.at[k],
            device_id={"img": peers[k]},
            device_id_type=MESH,
        )

    turned[...] = value_ref[...].T
    gram_slots[others] = jnp.dot(turned[...], value_ref[...], preferred_element_type=jnp.float32)
    greet("img", peers)
    grams = [remote(gram_slots.at[others], gram_slots.at[k], gram_send, gram_recv, k) for k in range(others)]
    raws = [remote(staged.at[k], raw_slots.at[k], raw_send, raw_recv, k) for k in range(others)]
    sends = [
        remote(solved_ref.at[pl.ds(pl.multiple_of(peers[k] * part, part), part)], row_slots.at[k], row_send, row_recv, k)
        for k in range(others)
    ]
    for copy in grams:
        copy.start()
    for k in range(others):
        raw = jnp.dot(turned[...], tile_ref[:, columns(peers[k])], preferred_element_type=jnp.float32)
        staged[k] = raw.astype(jnp.bfloat16)
        raws[k].start()
    mine = jnp.dot(turned[...], tile_ref[:, columns(me)], preferred_element_type=jnp.float32)
    for copy in grams:
        copy.wait_recv()
    total = jnp.zeros(inverse_ref.shape, jnp.float32)
    for sender in range(count):
        total = total + gram_slots[lax.rem(me + 2 * count - sender - 1, count)]
    factor_panels(scale, after, total, left, right, pivots, inverse_ref, min(32, total.shape[0]))
    for k, copy in enumerate(raws):
        copy.wait_recv()
        mine = mine + raw_slots[k].astype(jnp.float32)
    solved = jnp.dot(inverse_ref[...], mine, precision=lax.Precision.HIGHEST, preferred_element_type=jnp.float32) * root
    solved_ref[...] = solved.astype(jnp.bfloat16)
    for copy in sends:
        copy.start()
    out_ref[:, columns(me)] = solved_ref[pl.ds(pl.multiple_of(me * part, part), part), :].astype(jnp.float32)
    for k, copy in enumerate(sends):
        copy.wait_recv()
        sender = lax.rem(me + count - 1 - k, count)
        out_ref[:, columns(sender)] = row_slots[k].astype(jnp.float32)
    for copy in grams + raws + sends:
        copy.wait_send()


def finish(value, tiles, count, scale, after, root):
    rows, rank = value.shape
    feats = tiles.shape[1]
    others = max(count - 1, 1)
    span = feats // count
    part = rank // count
    square = pltpu.VMEM((rank, rank), jnp.float32)
    return pl.pallas_call(
        functools.partial(finish_kernel, count, scale, after, root),
        in_specs=[VMEM] * 2,
        out_specs=[VMEM] * 2,
        out_shape=[
            jax.ShapeDtypeStruct((rank, rank), jnp.float32),
            jax.ShapeDtypeStruct((part, feats), jnp.float32),
        ],
        scratch_shapes=[
            pltpu.VMEM((rank, rows), jnp.bfloat16),
            pltpu.VMEM((others + 1, rank, rank), jnp.float32),
            pltpu.VMEM((others, rank, span), jnp.bfloat16),
            pltpu.VMEM((others, rank, span), jnp.bfloat16),
            pltpu.VMEM((rank, span), jnp.bfloat16),
            pltpu.VMEM((others, part, span), jnp.bfloat16),
            square,
            square,
            square,
        ]
        + [pltpu.SemaphoreType.DMA((others,))] * 6,
        compiler_params=pltpu.CompilerParams(
            collective_id=2, has_side_effects=True, vmem_limit_bytes=20 << 20
        ),
    )(value, tiles)


def on_device(coeffs, triples, sketch):
    rows_here = coeffs.shape[0]
    feats_here = triples.shape[1]
    img_count = lax.axis_size("img")
    feat_count = lax.axis_size("feat")
    total_rows = rows_here * img_count
    total_feats = feats_here * feat_count
    tiles, value = gather_features(coeffs, triples, sketch, feat_count)
    sketch_scale = (1.5 / total_feats) ** 0.5
    inverse, projected = finish(
        value, tiles, img_count, sketch_scale * sketch_scale / total_rows, sketch_scale, total_rows**-0.5
    )
    basis = jnp.dot(value.astype(jnp.float32), inverse.T, precision=lax.Precision.HIGHEST)
    return (basis, projected)


def solution(mesh):
    in_specs = (P("img", "feat"), P(None, "feat"), P("feat", None))
    out_specs = (P("img", None), P("img", "feat"))
    return jax.shard_map(
        on_device, mesh=mesh, in_specs=in_specs, out_specs=out_specs, check_vma=False
    )
```

```python
import functools

import jax
import jax.numpy as jnp
from jax import lax
from jax.experimental import pallas as pl
from jax.experimental.pallas import tpu as pltpu
from jax.sharding import PartitionSpec as P

CHUNKS = 8
AHEAD = 2
SUB = 8
MESH = pl.DeviceIdType.MESH
VMEM = pl.BlockSpec(memory_space=pltpu.VMEM)
HBM = pl.BlockSpec(memory_space=pltpu.HBM)


def greet(axis, peers):
    barrier = pltpu.get_barrier_semaphore()
    for peer in peers:
        pl.semaphore_signal(barrier, inc=1, device_id={axis: peer}, device_id_type=MESH)
    pl.semaphore_wait(barrier, len(peers))


def gather_kernel(
    count, width, coeffs_hbm, triples_hbm, sketch_hbm, tile_ref, value_ref, triples_ref, sketch_ref, blocks, sel_ref,
    signs_ref, sum_ref, part_ref, slots, full_ref, own_sem, send_sem, recv_sem, to_sem, from_sem, out_sem, in_sem
):
    me = lax.axis_index("feat")
    rows, part = coeffs_hbm.shape
    step = rows // CHUNKS
    half = count * part // 2
    tiles = sketch_ref.shape[0] // width
    spans = ((0, half), (half, half), (2 * half, 2 * half))

    def build(index):
        start, depth = spans[index]

        def one(j, carry):
            cols = pl.ds(pl.multiple_of(j * width, width), width)
            levels = lax.broadcasted_iota(jnp.int32, (depth, width), 0)
            chosen = triples_ref[index : index + 1, cols]
            sel_ref[start : start + depth, cols] = jnp.where(levels == chosen, 1.0, 0.0).astype(jnp.bfloat16)
            if index == 2:
                signs_ref[cols, :] = sketch_ref[cols, :].astype(jnp.float32).astype(jnp.bfloat16)
            return carry

        lax.fori_loop(0, tiles, one, 0)

    own = pltpu.make_async_copy(coeffs_hbm, blocks.at[me], own_sem.at[0])
    own.start()
    triples_copy = pltpu.make_async_copy(triples_hbm, triples_ref, own_sem.at[1])
    triples_copy.start()
    sketch_copy = pltpu.make_async_copy(sketch_hbm, sketch_ref, own_sem.at[2])
    sketch_copy.start()
    peers = peers_of(me, count)
    piece = step // count
    greet("feat", peers)
    own.wait()
    triples_copy.wait()

    def copy(side, hop, chunk, source, target):
        span = blocks.at[source, pl.ds(pl.multiple_of(chunk * step, step), step)]
        return pltpu.make_async_remote_copy(
            src_ref=span,
            dst_ref=span,
            send_sem=send_sem.at[side, hop, chunk],
            recv_sem=recv_sem.at[side, hop, chunk],
            device_id={"feat": target},
            device_id_type=MESH,
        )

    def rows_of(chunk, owner):
        return pl.ds(pl.multiple_of(chunk * step + owner * piece, piece), piece)

    def reduce_copy(k, chunk):
        return pltpu.make_async_remote_copy(
            src_ref=part_ref.at[rows_of(chunk, peers[k])],
            dst_ref=slots.at[k, chunk],
            send_sem=to_sem.at[k, chunk],
            recv_sem=from_sem.at[k, chunk],
            device_id={"feat": peers[k]},
            device_id_type=MESH,
        )

    def spread_copy(k, chunk, owner):
        span = full_ref.at[rows_of(chunk, owner)]
        return pltpu.make_async_remote_copy(
            src_ref=span,
            dst_ref=span,
            send_sem=out_sem.at[k, chunk],
            recv_sem=in_sem.at[k, chunk],
            device_id={"feat": peers[k]},
            device_id_type=MESH,
        )

    def send_own(chunk, live):
        @pl.when(live & (me < count - 1))
        def _():
            copy(0, 0, chunk, me, me + 1).start()

        @pl.when(live & (me > 0))
        def _():
            copy(1, 0, chunk, me, me - 1).start()

    for chunk in range(AHEAD):
        send_own(chunk, True)

    def one_round(turn, carry):
        for hop in range(count):
            chunk = turn - hop
            live = (chunk >= 0) & (chunk < CHUNKS)
            if hop > 0:

                @pl.when(live & (me >= hop))
                def _():
                    copy(0, hop - 1, chunk, me - hop, me - 1).wait_recv()

                @pl.when(live & (me + hop < count))
                def _():
                    copy(1, hop - 1, chunk, me + hop, me + 1).wait_recv()

            if 0 < hop < count - 1:

                @pl.when(live & (me >= hop) & (me < count - 1))
                def _():
                    copy(0, hop, chunk, me - hop, me + 1).start()

                @pl.when(live & (me + hop < count) & (me > 0))
                def _():
                    copy(1, hop, chunk, me + hop, me - 1).start()

        send_own(turn + AHEAD, (turn + AHEAD) < CHUNKS)

        for index in range(3):

            @pl.when(turn == min(index, count - 2))
            def _():
                if index == 2:
                    sketch_copy.wait()
                build(index)

        base = turn - (count - 1)

        @pl.when((base >= 1) & (base <= CHUNKS))
        def _():
            for k in range(count - 1):
                reduce_copy(k, base - 1).start()

        @pl.when(base >= 2)
        def _():
            for k in range(count - 1):
                spread_copy(k, base - 2, me).start()

        @pl.when((base >= 0) & (base < CHUNKS))
        def _():
            first_row = pl.multiple_of(base * step, step)
            here = pl.ds(first_row, step)
            sum_ref[...] = jnp.zeros(sum_ref.shape, jnp.float32)
            low = jnp.concatenate([blocks[s, here, :] for s in range(count // 2)], axis=1)
            high = jnp.concatenate([blocks[s, here, :] for s in range(count // 2, count)], axis=1)
            full = jnp.concatenate([low, high], axis=1)

            def one_tile(j, unused):
                cols = pl.ds(pl.multiple_of(j * width, width), width)
                first = jnp.dot(low, sel_ref[:half, cols], preferred_element_type=jnp.float32)
                second = jnp.dot(low, sel_ref[half : 2 * half, cols], preferred_element_type=jnp.float32)
                third = jnp.dot(full, sel_ref[2 * half :, cols], preferred_element_type=jnp.float32)
                tile = (first * second * third).astype(jnp.bfloat16)
                tile_ref[here, cols] = tile
                sum_ref[...] += jnp.dot(tile, signs_ref[cols, :], preferred_element_type=jnp.float32)
                return unused

            lax.fori_loop(0, tiles, one_tile, 0, unroll=2)
            part_ref[here, :] = sum_ref[...].astype(jnp.bfloat16)

        @pl.when((base >= 1) & (base <= CHUNKS))
        def _():
            mine = rows_of(base - 1, me)
            total = part_ref[mine, :].astype(jnp.float32)
            for k in range(count - 1):
                reduce_copy(k, base - 1).wait_recv()
                total = total + slots[k, base - 1].astype(jnp.float32)
            full_ref[mine, :] = total.astype(jnp.bfloat16)

        return carry

    lax.fori_loop(0, CHUNKS + count + 1, one_round, 0)

    def drain(chunk, carry):
        for k in range(count - 1):
            spread_copy(k, chunk, lax.rem(me + count - 1 - k, count)).wait_recv()
            spread_copy(k, chunk, me).wait_send()
            reduce_copy(k, chunk).wait_send()
        for hop in range(count - 1):

            @pl.when((me >= hop) & (me < count - 1))
            def _():
                copy(0, hop, chunk, me - hop, me + 1).wait_send()

            @pl.when((me + hop < count) & (me > 0))
            def _():
                copy(1, hop, chunk, me + hop, me - 1).wait_send()

        return carry

    lax.fori_loop(0, CHUNKS, drain, 0)
    value_ref[...] = full_ref[...]


def gather_features(coeffs, triples, sketch, count):
    rows, part = coeffs.shape
    feats, rank = sketch.shape
    hops = max(count - 1, 1)
    step = rows // CHUNKS
    return pl.pallas_call(
        functools.partial(gather_kernel, count, min(1024, feats)),
        in_specs=[HBM] * 3,
        out_specs=[VMEM] * 2,
        out_shape=[
            jax.ShapeDtypeStruct((rows, feats), jnp.bfloat16),
            jax.ShapeDtypeStruct((rows, rank), jnp.bfloat16),
        ],
        scratch_shapes=[
            pltpu.VMEM(triples.shape, jnp.int32),
            pltpu.VMEM((feats, rank), jnp.int32),
            pltpu.VMEM((count, rows, part), jnp.bfloat16),
            pltpu.VMEM((2 * count * part, feats), jnp.bfloat16),
            pltpu.VMEM((feats, rank), jnp.bfloat16),
            pltpu.VMEM((step, rank), jnp.float32),
            pltpu.VMEM((rows, rank), jnp.bfloat16),
            pltpu.VMEM((hops, CHUNKS, step // count, rank), jnp.bfloat16),
            pltpu.VMEM((rows, rank), jnp.bfloat16),
            pltpu.SemaphoreType.DMA((3,)),
            pltpu.SemaphoreType.DMA((2, hops, CHUNKS)),
            pltpu.SemaphoreType.DMA((2, hops, CHUNKS)),
        ]
        + [pltpu.SemaphoreType.DMA((hops, CHUNKS))] * 4,
        compiler_params=pltpu.CompilerParams(
            collective_id=0, has_side_effects=True, vmem_limit_bytes=24 << 20
        ),
    )(*(pltpu.with_memory_space_constraint(a, pltpu.HBM) for a in (coeffs, triples, sketch)))


def peers_of(me, count):
    return [lax.rem(me + k, count) for k in range(1, count)]


def factor_panels(scale, after, gram, left, right, pivots, out_ref, width):
    size = gram.shape[0]
    rows = lax.broadcasted_iota(jnp.int32, (width, size), 0)
    lanes = lax.broadcasted_iota(jnp.int32, (width, size), 1)
    left[...] = gram * scale
    whole_rows = lax.broadcasted_iota(jnp.int32, (size, size), 0)
    whole_lanes = lax.broadcasted_iota(jnp.int32, (size, size), 1)
    right[...] = jnp.where(whole_rows == whole_lanes, 1.0, 0.0)

    def panel(p, carry):
        first = pl.multiple_of(p * width, width)
        here = pl.ds(first, width)
        block = left[here, :]
        twin = right[here, :]
        inverse = jnp.zeros((width, size), jnp.float32)
        for start in range(0, width, SUB):
            columns = [
                jnp.take_along_axis(block, jnp.full((width, size), first + start + j, jnp.int32), axis=1)
                for j in range(SUB)
            ]
            for j in range(SUB):
                at = start + j
                ratio = 1.0 / columns[j][at : at + 1, :]
                inverse = jnp.where(rows == at, ratio, inverse)
                if at + 1 < width:
                    factor = jnp.where(rows > at, columns[j] * ratio, 0.0)
                    for m in range(j + 1, SUB):
                        columns[m] = columns[m] - factor * columns[m][at : at + 1, :]
                    block = block - factor * block[at : at + 1, :]
                    twin = twin - factor * twin[at : at + 1, :]
        pivots[here, :] = inverse
        right[here, :] = twin

        @pl.when(p + 1 < size // width)
        def _():
            factor = jnp.where(lanes >= first + width, block * inverse, 0.0)
            across = (((0,), (0,)), ((), ()))
            exact = lax.Precision.HIGHEST
            left[...] -= lax.dot_general(factor, block, across, precision=exact, preferred_element_type=jnp.float32)
            right[...] -= lax.dot_general(factor, twin, across, precision=exact, preferred_element_type=jnp.float32)

        return carry

    lax.fori_loop(0, size // width, panel, 0)
    out_ref[...] = right[...] * (after * jnp.sqrt(pivots[...]))


def finish_kernel(
    count, scale, after, root, value_ref, tile_ref, inverse_ref, out_ref, turned, gram_slots, staged, raw_slots,
    solved_ref, row_slots, left, right, pivots, gram_send, gram_recv, raw_send, raw_recv, row_send, row_recv
):
    me = lax.axis_index("img")
    peers = peers_of(me, count)
    others = count - 1
    span = tile_ref.shape[1] // count
    part = out_ref.shape[0]

    def columns(owner):
        return pl.ds(pl.multiple_of(owner * span, span), span)

    def remote(source, target, send, recv, k):
        return pltpu.make_async_remote_copy(
            src_ref=source,
            dst_ref=target,
            send_sem=send.at[k],
            recv_sem=recv.at[k],
            device_id={"img": peers[k]},
            device_id_type=MESH,
        )

    turned[...] = value_ref[...].T
    gram_slots[others] = jnp.dot(turned[...], value_ref[...], preferred_element_type=jnp.float32)
    greet("img", peers)
    grams = [remote(gram_slots.at[others], gram_slots.at[k], gram_send, gram_recv, k) for k in range(others)]
    raws = [remote(staged.at[k], raw_slots.at[k], raw_send, raw_recv, k) for k in range(others)]
    sends = [
        remote(solved_ref.at[pl.ds(pl.multiple_of(peers[k] * part, part), part)], row_slots.at[k], row_send, row_recv, k)
        for k in range(others)
    ]
    for copy in grams:
        copy.start()
    for k in range(others):
        raw = jnp.dot(turned[...], tile_ref[:, columns(peers[k])], preferred_element_type=jnp.float32)
        staged[k] = raw.astype(jnp.bfloat16)
        raws[k].start()
    mine = jnp.dot(turned[...], tile_ref[:, columns(me)], preferred_element_type=jnp.float32)
    for copy in grams:
        copy.wait_recv()
    total = jnp.zeros(inverse_ref.shape, jnp.float32)
    for sender in range(count):
        total = total + gram_slots[lax.rem(me + 2 * count - sender - 1, count)]
    factor_panels(scale, after, total, left, right, pivots, inverse_ref, min(32, total.shape[0]))
    for k, copy in enumerate(raws):
        copy.wait_recv()
        mine = mine + raw_slots[k].astype(jnp.float32)
    solved = jnp.dot(inverse_ref[...], mine, precision=lax.Precision.HIGHEST, preferred_element_type=jnp.float32) * root
    solved_ref[...] = solved.astype(jnp.bfloat16)
    for copy in sends:
        copy.start()
    out_ref[:, columns(me)] = solved_ref[pl.ds(pl.multiple_of(me * part, part), part), :].astype(jnp.float32)
    for k, copy in enumerate(sends):
        copy.wait_recv()
        sender = lax.rem(me + count - 1 - k, count)
        out_ref[:, columns(sender)] = row_slots[k].astype(jnp.float32)
    for copy in grams + raws + sends:
        copy.wait_send()


def finish(value, tiles, count, scale, after, root):
    rows, rank = value.shape
    feats = tiles.shape[1]
    others = max(count - 1, 1)
    span = feats // count
    part = rank // count
    square = pltpu.VMEM((rank, rank), jnp.float32)
    return pl.pallas_call(
        functools.partial(finish_kernel, count, scale, after, root),
        in_specs=[VMEM] * 2,
        out_specs=[VMEM] * 2,
        out_shape=[
            jax.ShapeDtypeStruct((rank, rank), jnp.float32),
            jax.ShapeDtypeStruct((part, feats), jnp.float32),
        ],
        scratch_shapes=[
            pltpu.VMEM((rank, rows), jnp.bfloat16),
            pltpu.VMEM((others + 1, rank, rank), jnp.float32),
            pltpu.VMEM((others, rank, span), jnp.bfloat16),
            pltpu.VMEM((others, rank, span), jnp.bfloat16),
            pltpu.VMEM((rank, span), jnp.bfloat16),
            pltpu.VMEM((others, part, span), jnp.bfloat16),
            square,
            square,
            square,
        ]
        + [pltpu.SemaphoreType.DMA((others,))] * 6,
        compiler_params=pltpu.CompilerParams(
            collective_id=2, has_side_effects=True, vmem_limit_bytes=12 << 20
        ),
    )(value, tiles)


def on_device(coeffs, triples, sketch):
    rows_here = coeffs.shape[0]
    feats_here = triples.shape[1]
    img_count = lax.axis_size("img")
    feat_count = lax.axis_size("feat")
    total_rows = rows_here * img_count
    total_feats = feats_here * feat_count
    tiles, value = gather_features(coeffs, triples, sketch, feat_count)
    sketch_scale = (1.5 / total_feats) ** 0.5
    inverse, projected = finish(
        value, tiles, img_count, sketch_scale * sketch_scale / total_rows, sketch_scale, total_rows**-0.5
    )
    basis = jnp.dot(value.astype(jnp.float32), inverse.T, precision=lax.Precision.HIGHEST)
    return (basis, projected)


def solution(mesh):
    in_specs = (P("img", "feat"), P(None, "feat"), P("feat", None))
    out_specs = (P("img", None), P("img", "feat"))
    return jax.shard_map(
        on_device, mesh=mesh, in_specs=in_specs, out_specs=out_specs, check_vma=False
    )
```

```python
import functools

import jax
import jax.numpy as jnp
from jax import lax
from jax.experimental import pallas as pl
from jax.experimental.pallas import tpu as pltpu
from jax.sharding import PartitionSpec as P

CHUNKS = 8
AHEAD = 2
SUB = 8
PANEL = 32
MESH = pl.DeviceIdType.MESH
VMEM = pl.BlockSpec(memory_space=pltpu.VMEM)
HBM = pl.BlockSpec(memory_space=pltpu.HBM)


def greet(groups):
    barrier = pltpu.get_barrier_semaphore()
    for axis, peers in groups:
        for peer in peers:
            pl.semaphore_signal(barrier, inc=1, device_id={axis: peer}, device_id_type=MESH)
    pl.semaphore_wait(barrier, sum(len(peers) for axis, peers in groups))


def peers_of(me, count):
    return [lax.rem(me + k, count) for k in range(1, count)]


def factor_panels(scale, after, gram, left, right, pivots, out_ref, width):
    size = gram.shape[0]
    rows = lax.broadcasted_iota(jnp.int32, (width, size), 0)
    lanes = lax.broadcasted_iota(jnp.int32, (width, size), 1)
    left[...] = gram * scale
    whole_rows = lax.broadcasted_iota(jnp.int32, (size, size), 0)
    whole_lanes = lax.broadcasted_iota(jnp.int32, (size, size), 1)
    right[...] = jnp.where(whole_rows == whole_lanes, 1.0, 0.0)

    def panel(p, carry):
        first = pl.multiple_of(p * width, width)
        here = pl.ds(first, width)
        block = left[here, :]
        twin = right[here, :]
        inverse = jnp.zeros((width, size), jnp.float32)
        for start in range(0, width, SUB):
            columns = [
                jnp.take_along_axis(block, jnp.full((width, size), first + start + j, jnp.int32), axis=1)
                for j in range(SUB)
            ]
            for j in range(SUB):
                at = start + j
                ratio = 1.0 / columns[j][at : at + 1, :]
                inverse = jnp.where(rows == at, ratio, inverse)
                if at + 1 < width:
                    factor = jnp.where(rows > at, columns[j] * ratio, 0.0)
                    for m in range(j + 1, SUB):
                        columns[m] = columns[m] - factor * columns[m][at : at + 1, :]
                    block = block - factor * block[at : at + 1, :]
                    twin = twin - factor * twin[at : at + 1, :]
        pivots[here, :] = inverse
        right[here, :] = twin

        @pl.when(p + 1 < size // width)
        def _():
            factor = jnp.where(lanes >= first + width, block * inverse, 0.0)
            across = (((0,), (0,)), ((), ()))
            exact = lax.Precision.HIGHEST
            left[...] -= lax.dot_general(factor, block, across, precision=exact, preferred_element_type=jnp.float32)
            right[...] -= lax.dot_general(factor, twin, across, precision=exact, preferred_element_type=jnp.float32)

        return carry

    lax.fori_loop(0, size // width, panel, 0)
    out_ref[...] = right[...] * (after * jnp.sqrt(pivots[...]))


def whole_kernel(
    count, images, width, scale, after, root, coeffs_hbm, triples_hbm, sketch_hbm, value_ref, inverse_ref, out_ref,
    triples_ref, sketch_ref, tile_ref, blocks, sel_ref, signs_ref, sum_ref, part_ref, slots, full_ref, gram_ref,
    raw_ref, pair_gram, chip_gram, pair_staged, pair_raw, chip_staged, chip_raw, solved_ref, row_slots, left, right,
    pivots, own_sem, send_sem, recv_sem, to_sem, from_sem, out_sem, in_sem, gram_send, gram_recv, pair_send, pair_recv,
    chip_send, chip_recv, row_send, row_recv
):
    me = lax.axis_index("feat")
    spot = lax.axis_index("img")
    rows, part = coeffs_hbm.shape
    feats = triples_ref.shape[1]
    step = rows // CHUNKS
    half = count * part // 2
    tiles = feats // width
    spans = ((0, half), (half, half), (2 * half, 2 * half))

    def build(index):
        start, depth = spans[index]

        def one(j, carry):
            cols = pl.ds(pl.multiple_of(j * width, width), width)
            levels = lax.broadcasted_iota(jnp.int32, (depth, width), 0)
            chosen = triples_ref[index : index + 1, cols]
            sel_ref[start : start + depth, cols] = jnp.where(levels == chosen, 1.0, 0.0).astype(jnp.bfloat16)
            if index == 2:
                signs_ref[cols, :] = sketch_ref[cols, :].astype(jnp.float32).astype(jnp.bfloat16)
            return carry

        lax.fori_loop(0, tiles, one, 0)

    own = pltpu.make_async_copy(coeffs_hbm, blocks.at[me], own_sem.at[0])
    own.start()
    triples_copy = pltpu.make_async_copy(triples_hbm, triples_ref, own_sem.at[1])
    triples_copy.start()
    sketch_copy = pltpu.make_async_copy(sketch_hbm, sketch_ref, own_sem.at[2])
    sketch_copy.start()
    peers = peers_of(spot, images)
    greet((("feat", peers_of(me, count)), ("img", peers)))
    own.wait()
    triples_copy.wait()

    def copy(side, hop, chunk, source, target):
        span = blocks.at[source, pl.ds(pl.multiple_of(chunk * step, step), step)]
        return pltpu.make_async_remote_copy(
            src_ref=span,
            dst_ref=span,
            send_sem=send_sem.at[side, hop, chunk],
            recv_sem=recv_sem.at[side, hop, chunk],
            device_id={"feat": target},
            device_id_type=MESH,
        )

    owners = (count // 2 - 1, count // 2)
    piece = step // len(owners)

    def rows_of(chunk, o):
        return pl.ds(pl.multiple_of(chunk * step + o * piece, piece), piece)

    def reduce_copy(o, chunk, sender):
        return pltpu.make_async_remote_copy(
            src_ref=part_ref.at[rows_of(chunk, o)],
            dst_ref=slots.at[sender, chunk],
            send_sem=to_sem.at[o, chunk],
            recv_sem=from_sem.at[sender, chunk],
            device_id={"feat": owners[o]},
            device_id_type=MESH,
        )

    def spread_copy(o, chunk, target):
        span = full_ref.at[rows_of(chunk, o)]
        return pltpu.make_async_remote_copy(
            src_ref=span,
            dst_ref=span,
            send_sem=out_sem.at[target, chunk],
            recv_sem=in_sem.at[o, chunk],
            device_id={"feat": target},
            device_id_type=MESH,
        )

    def send_own(chunk, live):
        @pl.when(live & (me < count - 1))
        def _():
            copy(0, 0, chunk, me, me + 1).start()

        @pl.when(live & (me > 0))
        def _():
            copy(1, 0, chunk, me, me - 1).start()

    for chunk in range(AHEAD):
        send_own(chunk, True)
    gram_ref[...] = jnp.zeros(gram_ref.shape, jnp.float32)
    raw_ref[...] = jnp.zeros(raw_ref.shape, jnp.float32)

    def one_round(turn, carry):
        for hop in range(count):
            chunk = turn - hop
            live = (chunk >= 0) & (chunk < CHUNKS)
            if hop > 0:

                @pl.when(live & (me >= hop))
                def _():
                    copy(0, hop - 1, chunk, me - hop, me - 1).wait_recv()

                @pl.when(live & (me + hop < count))
                def _():
                    copy(1, hop - 1, chunk, me + hop, me + 1).wait_recv()

            if 0 < hop < count - 1:

                @pl.when(live & (me >= hop) & (me < count - 1))
                def _():
                    copy(0, hop, chunk, me - hop, me + 1).start()

                @pl.when(live & (me + hop < count) & (me > 0))
                def _():
                    copy(1, hop, chunk, me + hop, me - 1).start()

        send_own(turn + AHEAD, (turn + AHEAD) < CHUNKS)
        for index in range(3):

            @pl.when(turn == min(index, count - 2))
            def _():
                if index == 2:
                    sketch_copy.wait()
                build(index)

        base = turn - (count - 1)
        for o, owner in enumerate(owners):

            @pl.when((base >= 1) & (base <= CHUNKS) & (me != owner))
            def _():
                reduce_copy(o, base - 1, me).start()

            @pl.when((base >= 2) & (me == owner))
            def _():
                for target in range(count):
                    if target != owner:
                        spread_copy(o, base - 2, target).start()

        @pl.when((base >= 0) & (base < CHUNKS))
        def _():
            here = pl.ds(pl.multiple_of(base * step, step), step)
            sum_ref[...] = jnp.zeros(sum_ref.shape, jnp.float32)
            low = jnp.concatenate([blocks[s, here, :] for s in range(count // 2)], axis=1)
            high = jnp.concatenate([blocks[s, here, :] for s in range(count // 2, count)], axis=1)
            full = jnp.concatenate([low, high], axis=1)

            def one_tile(j, unused):
                cols = pl.ds(pl.multiple_of(j * width, width), width)
                first = jnp.dot(low, sel_ref[:half, cols], preferred_element_type=jnp.float32)
                second = jnp.dot(low, sel_ref[half : 2 * half, cols], preferred_element_type=jnp.float32)
                third = jnp.dot(full, sel_ref[2 * half :, cols], preferred_element_type=jnp.float32)
                tile = (first * second * third).astype(jnp.bfloat16)
                tile_ref[here, cols] = tile
                sum_ref[...] += jnp.dot(tile, signs_ref[cols, :], preferred_element_type=jnp.float32)
                return unused

            lax.fori_loop(0, tiles, one_tile, 0, unroll=2)
            part_ref[here, :] = sum_ref[...].astype(jnp.bfloat16)

        for o, owner in enumerate(owners):

            @pl.when((base >= 1) & (base <= CHUNKS) & (me == owner))
            def _():
                mine = rows_of(base - 1, o)
                total = part_ref[mine, :].astype(jnp.float32)
                for sender in range(count):
                    if sender != owner:
                        reduce_copy(o, base - 1, sender).wait_recv()
                        total = total + slots[sender, base - 1].astype(jnp.float32)
                full_ref[mine, :] = total.astype(jnp.bfloat16)

        for o, owner in enumerate(owners):

            @pl.when((base >= 2) & (me != owner))
            def _():
                spread_copy(o, base - 2, me).wait_recv()

        @pl.when(base >= 2)
        def _():
            here = pl.ds(pl.multiple_of((base - 2) * step, step), step)
            value = full_ref[here, :]
            turned = value.T
            gram_ref[...] += jnp.dot(turned, value, preferred_element_type=jnp.float32)

            def one_tile(j, unused):
                cols = pl.ds(pl.multiple_of(j * width, width), width)
                raw_ref[:, cols] += jnp.dot(turned, tile_ref[here, cols], preferred_element_type=jnp.float32)
                return unused

            lax.fori_loop(0, tiles, one_tile, 0)

        return carry

    lax.fori_loop(0, CHUNKS + count + 1, one_round, 0)

    side = lax.rem(spot, 2)
    pairs = images // 2
    chips = [lax.rem(spot + 2 * k, images) for k in range(1, pairs)]
    span = feats // images
    rank_part = out_ref.shape[0]

    def columns(owner):
        return pl.ds(pl.multiple_of(owner * span, span), span)

    def remote(source, target, send, recv, device):
        return pltpu.make_async_remote_copy(
            src_ref=source, dst_ref=target, send_sem=send, recv_sem=recv, device_id={"img": device}, device_id_type=MESH
        )

    twin = spot + 1 - 2 * side
    gram_pair = remote(gram_ref, pair_gram, gram_send.at[0], gram_recv.at[0], twin)
    gram_pair.start()
    pair_copies = []
    for m in range(pairs):
        pair_staged[m] = raw_ref[:, columns(2 * m + 1 - side)].astype(jnp.bfloat16)
        pair_copies.append(remote(pair_staged.at[m], pair_raw.at[m], pair_send.at[m], pair_recv.at[m], twin))
        pair_copies[-1].start()
    gram_pair.wait_recv()
    chip_gram[0] = gram_ref[...] + pair_gram[...]
    gram_copies = [
        remote(chip_gram.at[0], chip_gram.at[k + 1], gram_send.at[k + 1], gram_recv.at[k + 1], chip)
        for k, chip in enumerate(chips)
    ]
    for one in gram_copies:
        one.start()
    for one in pair_copies:
        one.wait_recv()
    chip_copies = []
    for k, chip in enumerate(chips):
        both = raw_ref[:, columns(chip)] + pair_raw[lax.div(chip, 2)].astype(jnp.float32)
        chip_staged[k] = both.astype(jnp.bfloat16)
        chip_copies.append(remote(chip_staged.at[k], chip_raw.at[k], chip_send.at[k], chip_recv.at[k], chip))
        chip_copies[-1].start()
    for one in gram_copies:
        one.wait_recv()
    total = jnp.zeros(gram_ref.shape, jnp.float32)
    for chip in range(pairs):
        total = total + chip_gram[lax.rem(lax.div(spot, 2) + pairs - chip, pairs)]
    factor_panels(scale, after, total, left, right, pivots, inverse_ref, min(PANEL, total.shape[0]))
    mine = raw_ref[:, columns(spot)] + pair_raw[lax.div(spot, 2)].astype(jnp.float32)
    for k, one in enumerate(chip_copies):
        one.wait_recv()
        mine = mine + chip_raw[k].astype(jnp.float32)
    solved = jnp.dot(inverse_ref[...], mine, precision=lax.Precision.HIGHEST, preferred_element_type=jnp.float32) * root
    solved_ref[...] = solved.astype(jnp.bfloat16)

    def ranks(owner):
        return pl.ds(pl.multiple_of(owner * rank_part, rank_part), rank_part)

    row_copies = [
        remote(solved_ref.at[ranks(peer)], row_slots.at[k], row_send.at[k], row_recv.at[k], peer)
        for k, peer in enumerate(peers)
    ]
    for one in row_copies:
        one.start()
    value_ref[...] = full_ref[...]
    out_ref[:, columns(spot)] = solved_ref[ranks(spot), :].astype(jnp.float32)

    def drain(chunk, carry):
        for o, owner in enumerate(owners):

            @pl.when(me != owner)
            def _():
                reduce_copy(o, chunk, me).wait_send()

            @pl.when(me == owner)
            def _():
                for target in range(count):
                    if target != owner:
                        spread_copy(o, chunk, target).wait_send()

        for hop in range(count - 1):

            @pl.when((me >= hop) & (me < count - 1))
            def _():
                copy(0, hop, chunk, me - hop, me + 1).wait_send()

            @pl.when((me + hop < count) & (me > 0))
            def _():
                copy(1, hop, chunk, me + hop, me - 1).wait_send()

        return carry

    lax.fori_loop(0, CHUNKS, drain, 0)
    for k, one in enumerate(row_copies):
        one.wait_recv()
        out_ref[:, columns(lax.rem(spot + images - 1 - k, images))] = row_slots[k].astype(jnp.float32)
    for one in [gram_pair] + pair_copies + gram_copies + chip_copies + row_copies:
        one.wait_send()


def factor_and_project(coeffs, triples, sketch, count, images, scale, after, root):
    rows, part = coeffs.shape
    feats, rank = sketch.shape
    hops = max(count - 1, 1)
    step = rows // CHUNKS
    pairs = images // 2
    span = feats // images
    rank_part = rank // images
    square = pltpu.VMEM((rank, rank), jnp.float32)
    dma = pltpu.SemaphoreType.DMA
    return pl.pallas_call(
        functools.partial(whole_kernel, count, images, min(1024, feats), scale, after, root),
        in_specs=[HBM] * 3,
        out_specs=[VMEM] * 3,
        out_shape=[
            jax.ShapeDtypeStruct((rows, rank), jnp.bfloat16),
            jax.ShapeDtypeStruct((rank, rank), jnp.float32),
            jax.ShapeDtypeStruct((rank_part, feats), jnp.float32),
        ],
        scratch_shapes=[
            pltpu.VMEM(triples.shape, jnp.int32),
            pltpu.VMEM((feats, rank), jnp.int32),
            pltpu.VMEM((rows, feats), jnp.bfloat16),
            pltpu.VMEM((count, rows, part), jnp.bfloat16),
            pltpu.VMEM((2 * count * part, feats), jnp.bfloat16),
            pltpu.VMEM((feats, rank), jnp.bfloat16),
            pltpu.VMEM((step, rank), jnp.float32),
            pltpu.VMEM((rows, rank), jnp.bfloat16),
            pltpu.VMEM((count, CHUNKS, step // 2, rank), jnp.bfloat16),
            pltpu.VMEM((rows, rank), jnp.bfloat16),
            square,
            pltpu.VMEM((rank, feats), jnp.float32),
            square,
            pltpu.VMEM((pairs, rank, rank), jnp.float32),
            pltpu.VMEM((pairs, rank, span), jnp.bfloat16),
            pltpu.VMEM((pairs, rank, span), jnp.bfloat16),
            pltpu.VMEM((pairs - 1, rank, span), jnp.bfloat16),
            pltpu.VMEM((pairs - 1, rank, span), jnp.bfloat16),
            pltpu.VMEM((rank, span), jnp.bfloat16),
            pltpu.VMEM((images - 1, rank_part, span), jnp.bfloat16),
            square,
            square,
            square,
            dma((3,)),
            dma((2, hops, CHUNKS)),
            dma((2, hops, CHUNKS)),
            dma((2, CHUNKS)),
            dma((count, CHUNKS)),
            dma((count, CHUNKS)),
            dma((2, CHUNKS)),
        ]
        + [dma((pairs,))] * 4
        + [dma((pairs - 1,))] * 2
        + [dma((images - 1,))] * 2,
        compiler_params=pltpu.CompilerParams(
            collective_id=0, has_side_effects=True, vmem_limit_bytes=44 << 20
        ),
    )(*(pltpu.with_memory_space_constraint(array, pltpu.HBM) for array in (coeffs, triples, sketch)))


def on_device(coeffs, triples, sketch):
    rows_here = coeffs.shape[0]
    feats_here = triples.shape[1]
    img_count = lax.axis_size("img")
    feat_count = lax.axis_size("feat")
    total_rows = rows_here * img_count
    total_feats = feats_here * feat_count
    sketch_scale = (1.5 / total_feats) ** 0.5
    value, inverse, projected = factor_and_project(
        coeffs, triples, sketch, feat_count, img_count,
        sketch_scale * sketch_scale / total_rows, sketch_scale, total_rows**-0.5,
    )
    basis = jnp.dot(value.astype(jnp.float32), inverse.T, precision=lax.Precision.HIGHEST)
    return (basis, projected)


def solution(mesh):
    in_specs = (P("img", "feat"), P(None, "feat"), P("feat", None))
    out_specs = (P("img", None), P("img", "feat"))
    return jax.shard_map(
        on_device, mesh=mesh, in_specs=in_specs, out_specs=out_specs, check_vma=False
    )
```

```python
import functools

import jax
import jax.numpy as jnp
from jax import lax
from jax.experimental import pallas as pl
from jax.experimental.pallas import tpu as pltpu
from jax.sharding import PartitionSpec as P

CHUNKS = 8
AHEAD = 2
SUB = 8
PANEL = 32
MESH = pl.DeviceIdType.MESH
VMEM = pl.BlockSpec(memory_space=pltpu.VMEM)
HBM = pl.BlockSpec(memory_space=pltpu.HBM)


def greet(groups):
    barrier = pltpu.get_barrier_semaphore()
    for axis, peers in groups:
        for peer in peers:
            pl.semaphore_signal(barrier, inc=1, device_id={axis: peer}, device_id_type=MESH)
    pl.semaphore_wait(barrier, sum(len(peers) for axis, peers in groups))


def peers_of(me, count):
    return [lax.rem(me + k, count) for k in range(1, count)]


def factor_panels(scale, after, gram, left, right, pivots, out_ref, width):
    size = gram.shape[0]
    rows = lax.broadcasted_iota(jnp.int32, (width, size), 0)
    lanes = lax.broadcasted_iota(jnp.int32, (width, size), 1)
    left[...] = gram * scale
    whole_rows = lax.broadcasted_iota(jnp.int32, (size, size), 0)
    whole_lanes = lax.broadcasted_iota(jnp.int32, (size, size), 1)
    right[...] = jnp.where(whole_rows == whole_lanes, 1.0, 0.0)

    def panel(p, carry):
        first = pl.multiple_of(p * width, width)
        here = pl.ds(first, width)
        block = left[here, :]
        twin = right[here, :]
        inverse = jnp.zeros((width, size), jnp.float32)
        for start in range(0, width, SUB):
            columns = [
                jnp.take_along_axis(block, jnp.full((width, size), first + start + j, jnp.int32), axis=1)
                for j in range(SUB)
            ]
            for j in range(SUB):
                at = start + j
                ratio = 1.0 / columns[j][at : at + 1, :]
                inverse = jnp.where(rows == at, ratio, inverse)
                if at + 1 < width:
                    factor = jnp.where(rows > at, columns[j] * ratio, 0.0)
                    for m in range(j + 1, SUB):
                        columns[m] = columns[m] - factor * columns[m][at : at + 1, :]
                    block = block - factor * block[at : at + 1, :]
                    twin = twin - factor * twin[at : at + 1, :]
        pivots[here, :] = inverse
        right[here, :] = twin

        @pl.when(p + 1 < size // width)
        def _():
            factor = jnp.where(lanes >= first + width, block * inverse, 0.0)
            across = (((0,), (0,)), ((), ()))
            exact = lax.Precision.HIGHEST
            left[...] -= lax.dot_general(factor, block, across, precision=exact, preferred_element_type=jnp.float32)
            right[...] -= lax.dot_general(factor, twin, across, precision=exact, preferred_element_type=jnp.float32)

        return carry

    lax.fori_loop(0, size // width, panel, 0)
    out_ref[...] = right[...] * (after * jnp.sqrt(pivots[...]))


def whole_kernel(
    count, images, width, scale, after, root, coeffs_hbm, triples_hbm, sketch_hbm, value_ref, inverse_ref, out_ref,
    triples_ref, sketch_ref, tile_ref, blocks, sel_ref, signs_ref, sum_ref, part_ref, slots, full_ref, gram_ref,
    raw_ref, pair_gram, chip_gram, pair_staged, pair_raw, chip_staged, chip_raw, solved_ref, row_slots, left, right,
    pivots, own_sem, send_sem, recv_sem, to_sem, from_sem, out_sem, in_sem, gram_send, gram_recv, pair_send, pair_recv,
    chip_send, chip_recv, row_send, row_recv
):
    me = lax.axis_index("feat")
    spot = lax.axis_index("img")
    rows, part = coeffs_hbm.shape
    feats = triples_ref.shape[1]
    step = rows // CHUNKS
    half = count * part // 2
    tiles = feats // width
    spans = ((0, half), (half, half), (2 * half, 2 * half))

    def build(index):
        start, depth = spans[index]

        def one(j, carry):
            cols = pl.ds(pl.multiple_of(j * width, width), width)
            levels = lax.broadcasted_iota(jnp.int32, (depth, width), 0)
            chosen = triples_ref[index : index + 1, cols]
            sel_ref[start : start + depth, cols] = jnp.where(levels == chosen, 1.0, 0.0).astype(jnp.bfloat16)
            if index == 2:
                signs_ref[cols, :] = sketch_ref[cols, :].astype(jnp.float32).astype(jnp.bfloat16)
            return carry

        lax.fori_loop(0, tiles, one, 0)

    own = pltpu.make_async_copy(coeffs_hbm, blocks.at[me], own_sem.at[0])
    own.start()
    triples_copy = pltpu.make_async_copy(triples_hbm, triples_ref, own_sem.at[1])
    triples_copy.start()
    sketch_copy = pltpu.make_async_copy(sketch_hbm, sketch_ref, own_sem.at[2])
    sketch_copy.start()
    peers = peers_of(spot, images)
    greet((("feat", peers_of(me, count)), ("img", peers)))
    own.wait()
    triples_copy.wait()

    def copy(side, hop, chunk, source, target):
        span = blocks.at[source, pl.ds(pl.multiple_of(chunk * step, step), step)]
        return pltpu.make_async_remote_copy(
            src_ref=span,
            dst_ref=span,
            send_sem=send_sem.at[side, hop, chunk],
            recv_sem=recv_sem.at[side, hop, chunk],
            device_id={"feat": target},
            device_id_type=MESH,
        )

    owners = (count // 2 - 1, count // 2)
    piece = step // len(owners)

    def rows_of(chunk, o):
        return pl.ds(pl.multiple_of(chunk * step + o * piece, piece), piece)

    def reduce_copy(o, chunk, sender):
        return pltpu.make_async_remote_copy(
            src_ref=part_ref.at[rows_of(chunk, o)],
            dst_ref=slots.at[sender, chunk],
            send_sem=to_sem.at[o, chunk],
            recv_sem=from_sem.at[sender, chunk],
            device_id={"feat": owners[o]},
            device_id_type=MESH,
        )

    def spread_copy(o, chunk, target):
        span = full_ref.at[rows_of(chunk, o)]
        return pltpu.make_async_remote_copy(
            src_ref=span,
            dst_ref=span,
            send_sem=out_sem.at[target, chunk],
            recv_sem=in_sem.at[o, chunk],
            device_id={"feat": target},
            device_id_type=MESH,
        )

    def send_own(chunk, live):
        @pl.when(live & (me < count - 1))
        def _():
            copy(0, 0, chunk, me, me + 1).start()

        @pl.when(live & (me > 0))
        def _():
            copy(1, 0, chunk, me, me - 1).start()

    for chunk in range(AHEAD):
        send_own(chunk, True)
    gram_ref[...] = jnp.zeros(gram_ref.shape, jnp.float32)
    raw_ref[...] = jnp.zeros(raw_ref.shape, jnp.float32)

    def one_round(turn, carry):
        for hop in range(count):
            chunk = turn - hop
            live = (chunk >= 0) & (chunk < CHUNKS)
            if hop > 0:

                @pl.when(live & (me >= hop))
                def _():
                    copy(0, hop - 1, chunk, me - hop, me - 1).wait_recv()

                @pl.when(live & (me + hop < count))
                def _():
                    copy(1, hop - 1, chunk, me + hop, me + 1).wait_recv()

            if 0 < hop < count - 1:

                @pl.when(live & (me >= hop) & (me < count - 1))
                def _():
                    copy(0, hop, chunk, me - hop, me + 1).start()

                @pl.when(live & (me + hop < count) & (me > 0))
                def _():
                    copy(1, hop, chunk, me + hop, me - 1).start()

        send_own(turn + AHEAD, (turn + AHEAD) < CHUNKS)
        for index in range(3):

            @pl.when(turn == min(index, count - 2))
            def _():
                if index == 2:
                    sketch_copy.wait()
                build(index)

        base = turn - (count - 1)
        for o, owner in enumerate(owners):

            @pl.when((base >= 1) & (base <= CHUNKS) & (me != owner))
            def _():
                reduce_copy(o, base - 1, me).start()

            @pl.when((base >= 2) & (base <= CHUNKS + 1) & (me == owner))
            def _():
                mine = rows_of(base - 2, o)
                total = part_ref[mine, :].astype(jnp.float32)
                for sender in range(count):
                    if sender != owner:
                        reduce_copy(o, base - 2, sender).wait_recv()
                        total = total + slots[sender, base - 2].astype(jnp.float32)
                full_ref[mine, :] = total.astype(jnp.bfloat16)
                for target in range(count):
                    if target != owner:
                        spread_copy(o, base - 2, target).start()

        @pl.when((base >= 0) & (base < CHUNKS))
        def _():
            here = pl.ds(pl.multiple_of(base * step, step), step)
            sum_ref[...] = jnp.zeros(sum_ref.shape, jnp.float32)
            low = jnp.concatenate([blocks[s, here, :] for s in range(count // 2)], axis=1)
            high = jnp.concatenate([blocks[s, here, :] for s in range(count // 2, count)], axis=1)
            full = jnp.concatenate([low, high], axis=1)

            def one_tile(j, unused):
                cols = pl.ds(pl.multiple_of(j * width, width), width)
                first = jnp.dot(low, sel_ref[:half, cols], preferred_element_type=jnp.float32)
                second = jnp.dot(low, sel_ref[half : 2 * half, cols], preferred_element_type=jnp.float32)
                third = jnp.dot(full, sel_ref[2 * half :, cols], preferred_element_type=jnp.float32)
                tile = (first * second * third).astype(jnp.bfloat16)
                tile_ref[here, cols] = tile
                sum_ref[...] += jnp.dot(tile, signs_ref[cols, :], preferred_element_type=jnp.float32)
                return unused

            lax.fori_loop(0, tiles, one_tile, 0, unroll=2)
            part_ref[here, :] = sum_ref[...].astype(jnp.bfloat16)

        for o, owner in enumerate(owners):

            @pl.when((base >= 3) & (me != owner))
            def _():
                spread_copy(o, base - 3, me).wait_recv()

        @pl.when(base >= 3)
        def _():
            here = pl.ds(pl.multiple_of((base - 3) * step, step), step)
            value = full_ref[here, :]
            turned = value.T
            gram_ref[...] += jnp.dot(turned, value, preferred_element_type=jnp.float32)

            def one_tile(j, unused):
                cols = pl.ds(pl.multiple_of(j * width, width), width)
                raw_ref[:, cols] += jnp.dot(turned, tile_ref[here, cols], preferred_element_type=jnp.float32)
                return unused

            lax.fori_loop(0, tiles, one_tile, 0)

        return carry

    lax.fori_loop(0, CHUNKS + count + 2, one_round, 0)

    side = lax.rem(spot, 2)
    pairs = images // 2
    chips = [lax.rem(spot + 2 * k, images) for k in range(1, pairs)]
    span = feats // images
    rank_part = out_ref.shape[0]

    def columns(owner):
        return pl.ds(pl.multiple_of(owner * span, span), span)

    def remote(source, target, send, recv, device):
        return pltpu.make_async_remote_copy(
            src_ref=source, dst_ref=target, send_sem=send, recv_sem=recv, device_id={"img": device}, device_id_type=MESH
        )

    twin = spot + 1 - 2 * side
    gram_pair = remote(gram_ref, pair_gram, gram_send.at[0], gram_recv.at[0], twin)
    gram_pair.start()
    pair_copies = []
    for m in range(pairs):
        pair_staged[m] = raw_ref[:, columns(2 * m + 1 - side)].astype(jnp.bfloat16)
        pair_copies.append(remote(pair_staged.at[m], pair_raw.at[m], pair_send.at[m], pair_recv.at[m], twin))
        pair_copies[-1].start()
    gram_pair.wait_recv()
    chip_gram[0] = gram_ref[...] + pair_gram[...]
    gram_copies = [
        remote(chip_gram.at[0], chip_gram.at[k + 1], gram_send.at[k + 1], gram_recv.at[k + 1], chip)
        for k, chip in enumerate(chips)
    ]
    for one in gram_copies:
        one.start()
    for one in pair_copies:
        one.wait_recv()
    chip_copies = []
    for k, chip in enumerate(chips):
        both = raw_ref[:, columns(chip)] + pair_raw[lax.div(chip, 2)].astype(jnp.float32)
        chip_staged[k] = both.astype(jnp.bfloat16)
        chip_copies.append(remote(chip_staged.at[k], chip_raw.at[k], chip_send.at[k], chip_recv.at[k], chip))
        chip_copies[-1].start()
    for one in gram_copies:
        one.wait_recv()
    total = jnp.zeros(gram_ref.shape, jnp.float32)
    for chip in range(pairs):
        total = total + chip_gram[lax.rem(lax.div(spot, 2) + pairs - chip, pairs)]
    factor_panels(scale, after, total, left, right, pivots, inverse_ref, min(PANEL, total.shape[0]))
    mine = raw_ref[:, columns(spot)] + pair_raw[lax.div(spot, 2)].astype(jnp.float32)
    for k, one in enumerate(chip_copies):
        one.wait_recv()
        mine = mine + chip_raw[k].astype(jnp.float32)
    solved = jnp.dot(inverse_ref[...], mine, precision=lax.Precision.HIGHEST, preferred_element_type=jnp.float32) * root
    solved_ref[...] = solved.astype(jnp.bfloat16)

    def ranks(owner):
        return pl.ds(pl.multiple_of(owner * rank_part, rank_part), rank_part)

    row_copies = [
        remote(solved_ref.at[ranks(peer)], row_slots.at[k], row_send.at[k], row_recv.at[k], peer)
        for k, peer in enumerate(peers)
    ]
    for one in row_copies:
        one.start()
    value_ref[...] = full_ref[...]
    out_ref[:, columns(spot)] = solved_ref[ranks(spot), :].astype(jnp.float32)

    def drain(chunk, carry):
        for o, owner in enumerate(owners):

            @pl.when(me != owner)
            def _():
                reduce_copy(o, chunk, me).wait_send()

            @pl.when(me == owner)
            def _():
                for target in range(count):
                    if target != owner:
                        spread_copy(o, chunk, target).wait_send()

        for hop in range(count - 1):

            @pl.when((me >= hop) & (me < count - 1))
            def _():
                copy(0, hop, chunk, me - hop, me + 1).wait_send()

            @pl.when((me + hop < count) & (me > 0))
            def _():
                copy(1, hop, chunk, me + hop, me - 1).wait_send()

        return carry

    lax.fori_loop(0, CHUNKS, drain, 0)
    for k, one in enumerate(row_copies):
        one.wait_recv()
        out_ref[:, columns(lax.rem(spot + images - 1 - k, images))] = row_slots[k].astype(jnp.float32)
    for one in [gram_pair] + pair_copies + gram_copies + chip_copies + row_copies:
        one.wait_send()


def factor_and_project(coeffs, triples, sketch, count, images, scale, after, root):
    rows, part = coeffs.shape
    feats, rank = sketch.shape
    hops = max(count - 1, 1)
    step = rows // CHUNKS
    pairs = images // 2
    span = feats // images
    rank_part = rank // images
    square = pltpu.VMEM((rank, rank), jnp.float32)
    dma = pltpu.SemaphoreType.DMA
    return pl.pallas_call(
        functools.partial(whole_kernel, count, images, min(1024, feats), scale, after, root),
        in_specs=[HBM] * 3,
        out_specs=[VMEM] * 3,
        out_shape=[
            jax.ShapeDtypeStruct((rows, rank), jnp.bfloat16),
            jax.ShapeDtypeStruct((rank, rank), jnp.float32),
            jax.ShapeDtypeStruct((rank_part, feats), jnp.float32),
        ],
        scratch_shapes=[
            pltpu.VMEM(triples.shape, jnp.int32),
            pltpu.VMEM((feats, rank), jnp.int32),
            pltpu.VMEM((rows, feats), jnp.bfloat16),
            pltpu.VMEM((count, rows, part), jnp.bfloat16),
            pltpu.VMEM((2 * count * part, feats), jnp.bfloat16),
            pltpu.VMEM((feats, rank), jnp.bfloat16),
            pltpu.VMEM((step, rank), jnp.float32),
            pltpu.VMEM((rows, rank), jnp.bfloat16),
            pltpu.VMEM((count, CHUNKS, step // 2, rank), jnp.bfloat16),
            pltpu.VMEM((rows, rank), jnp.bfloat16),
            square,
            pltpu.VMEM((rank, feats), jnp.float32),
            square,
            pltpu.VMEM((pairs, rank, rank), jnp.float32),
            pltpu.VMEM((pairs, rank, span), jnp.bfloat16),
            pltpu.VMEM((pairs, rank, span), jnp.bfloat16),
            pltpu.VMEM((pairs - 1, rank, span), jnp.bfloat16),
            pltpu.VMEM((pairs - 1, rank, span), jnp.bfloat16),
            pltpu.VMEM((rank, span), jnp.bfloat16),
            pltpu.VMEM((images - 1, rank_part, span), jnp.bfloat16),
            square,
            square,
            square,
            dma((3,)),
            dma((2, hops, CHUNKS)),
            dma((2, hops, CHUNKS)),
            dma((2, CHUNKS)),
            dma((count, CHUNKS)),
            dma((count, CHUNKS)),
            dma((2, CHUNKS)),
        ]
        + [dma((pairs,))] * 4
        + [dma((pairs - 1,))] * 2
        + [dma((images - 1,))] * 2,
        compiler_params=pltpu.CompilerParams(
            collective_id=0, has_side_effects=True, vmem_limit_bytes=44 << 20
        ),
    )(*(pltpu.with_memory_space_constraint(array, pltpu.HBM) for array in (coeffs, triples, sketch)))


def on_device(coeffs, triples, sketch):
    rows_here = coeffs.shape[0]
    feats_here = triples.shape[1]
    img_count = lax.axis_size("img")
    feat_count = lax.axis_size("feat")
    total_rows = rows_here * img_count
    total_feats = feats_here * feat_count
    sketch_scale = (1.5 / total_feats) ** 0.5
    value, inverse, projected = factor_and_project(
        coeffs, triples, sketch, feat_count, img_count,
        sketch_scale * sketch_scale / total_rows, sketch_scale, total_rows**-0.5,
    )
    basis = jnp.dot(value.astype(jnp.float32), inverse.T, precision=lax.Precision.HIGHEST)
    return (basis, projected)


def solution(mesh):
    in_specs = (P("img", "feat"), P(None, "feat"), P("feat", None))
    out_specs = (P("img", None), P("img", "feat"))
    return jax.shard_map(
        on_device, mesh=mesh, in_specs=in_specs, out_specs=out_specs, check_vma=False
    )
```

```python
import functools

import jax
import jax.numpy as jnp
from jax import lax
from jax.experimental import pallas as pl
from jax.experimental.pallas import tpu as pltpu
from jax.sharding import PartitionSpec as P

CHUNKS = 8
AHEAD = (4, 1)
SUMMED = 5
SPREAD = 7
SUB = 8
PANEL = 32
MESH = pl.DeviceIdType.MESH
VMEM = pl.BlockSpec(memory_space=pltpu.VMEM)
HBM = pl.BlockSpec(memory_space=pltpu.HBM)


def greet(groups):
    barrier = pltpu.get_barrier_semaphore()
    for axis, peers in groups:
        for peer in peers:
            pl.semaphore_signal(barrier, inc=1, device_id={axis: peer}, device_id_type=MESH)
    pl.semaphore_wait(barrier, sum(len(peers) for axis, peers in groups))


def peers_of(me, count):
    return [lax.rem(me + k, count) for k in range(1, count)]


def factor_panels(scale, after, gram, left, right, pivots, out_ref, width):
    size = gram.shape[0]
    rows = lax.broadcasted_iota(jnp.int32, (width, size), 0)
    lanes = lax.broadcasted_iota(jnp.int32, (width, size), 1)
    left[...] = gram * scale
    whole_rows = lax.broadcasted_iota(jnp.int32, (size, size), 0)
    whole_lanes = lax.broadcasted_iota(jnp.int32, (size, size), 1)
    right[...] = jnp.where(whole_rows == whole_lanes, 1.0, 0.0)

    def panel(p, carry):
        first = pl.multiple_of(p * width, width)
        here = pl.ds(first, width)
        block = left[here, :]
        twin = right[here, :]
        inverse = jnp.zeros((width, size), jnp.float32)
        for start in range(0, width, SUB):
            columns = [
                jnp.take_along_axis(block, jnp.full((width, size), first + start + j, jnp.int32), axis=1)
                for j in range(SUB)
            ]
            for j in range(SUB):
                at = start + j
                ratio = 1.0 / columns[j][at : at + 1, :]
                inverse = jnp.where(rows == at, ratio, inverse)
                if at + 1 < width:
                    factor = jnp.where(rows > at, columns[j] * ratio, 0.0)
                    for m in range(j + 1, SUB):
                        columns[m] = columns[m] - factor * columns[m][at : at + 1, :]
                    block = block - factor * block[at : at + 1, :]
                    twin = twin - factor * twin[at : at + 1, :]
        pivots[here, :] = inverse
        right[here, :] = twin

        @pl.when(p + 1 < size // width)
        def _():
            factor = jnp.where(lanes >= first + width, block * inverse, 0.0)
            across = (((0,), (0,)), ((), ()))
            exact = lax.Precision.HIGHEST
            left[...] -= lax.dot_general(factor, block, across, precision=exact, preferred_element_type=jnp.float32)
            right[...] -= lax.dot_general(factor, twin, across, precision=exact, preferred_element_type=jnp.float32)

        return carry

    lax.fori_loop(0, size // width, panel, 0)
    out_ref[...] = right[...] * (after * jnp.sqrt(pivots[...]))


def whole_kernel(
    count, images, width, scale, after, root, coeffs_hbm, triples_hbm, sketch_hbm, value_ref, inverse_ref, out_ref,
    triples_ref, sketch_ref, tile_ref, blocks, sel_ref, signs_ref, sum_ref, part_ref, slots, full_ref, gram_ref,
    raw_ref, pair_gram, chip_gram, pair_staged, pair_raw, chip_staged, chip_raw, solved_ref, row_slots, left, right,
    pivots, own_sem, send_sem, recv_sem, to_sem, from_sem, out_sem, in_sem, gram_send, gram_recv, pair_send, pair_recv,
    chip_send, chip_recv, row_send, row_recv
):
    me = lax.axis_index("feat")
    spot = lax.axis_index("img")
    rows, part = coeffs_hbm.shape
    feats = triples_ref.shape[1]
    step = rows // CHUNKS
    half = count * part // 2
    tiles = feats // width
    spans = ((0, half), (half, half), (2 * half, 2 * half))

    def build(index):
        start, depth = spans[index]

        def one(j, carry):
            cols = pl.ds(pl.multiple_of(j * width, width), width)
            levels = lax.broadcasted_iota(jnp.int32, (depth, width), 0)
            chosen = triples_ref[index : index + 1, cols]
            sel_ref[start : start + depth, cols] = jnp.where(levels == chosen, 1.0, 0.0).astype(jnp.bfloat16)
            if index == 2:
                signs_ref[cols, :] = sketch_ref[cols, :].astype(jnp.float32).astype(jnp.bfloat16)
            return carry

        lax.fori_loop(0, tiles, one, 0)

    own = pltpu.make_async_copy(coeffs_hbm, blocks.at[me], own_sem.at[0])
    own.start()
    triples_copy = pltpu.make_async_copy(triples_hbm, triples_ref, own_sem.at[1])
    triples_copy.start()
    sketch_copy = pltpu.make_async_copy(sketch_hbm, sketch_ref, own_sem.at[2])
    sketch_copy.start()
    peers = peers_of(spot, images)
    greet((("feat", peers_of(me, count)), ("img", peers)))
    own.wait()
    triples_copy.wait()

    def copy(side, hop, chunk, source, target):
        span = blocks.at[source, pl.ds(pl.multiple_of(chunk * step, step), step)]
        return pltpu.make_async_remote_copy(
            src_ref=span,
            dst_ref=span,
            send_sem=send_sem.at[side, hop, chunk],
            recv_sem=recv_sem.at[side, hop, chunk],
            device_id={"feat": target},
            device_id_type=MESH,
        )

    owners = (count // 2 - 1, count // 2)
    piece = step // len(owners)

    def rows_of(chunk, o):
        return pl.ds(pl.multiple_of(chunk * step + o * piece, piece), piece)

    def reduce_copy(o, chunk, sender):
        return pltpu.make_async_remote_copy(
            src_ref=part_ref.at[rows_of(chunk, o)],
            dst_ref=slots.at[sender, chunk],
            send_sem=to_sem.at[o, chunk],
            recv_sem=from_sem.at[sender, chunk],
            device_id={"feat": owners[o]},
            device_id_type=MESH,
        )

    def spread_copy(o, chunk, target):
        span = full_ref.at[rows_of(chunk, o)]
        return pltpu.make_async_remote_copy(
            src_ref=span,
            dst_ref=span,
            send_sem=out_sem.at[target, chunk],
            recv_sem=in_sem.at[o, chunk],
            device_id={"feat": target},
            device_id_type=MESH,
        )

    def send_own(chunk, live):
        @pl.when(live & (me < count - 1))
        def _():
            copy(0, 0, chunk, me, me + 1).start()

        @pl.when(live & (me > 0))
        def _():
            copy(1, 0, chunk, me, me - 1).start()

    ahead = AHEAD[0] + (AHEAD[1] - AHEAD[0]) * lax.rem(spot, 2)
    for chunk in range(max(AHEAD)):
        send_own(chunk, chunk < ahead)
    gram_ref[...] = jnp.zeros(gram_ref.shape, jnp.float32)
    raw_ref[...] = jnp.zeros(raw_ref.shape, jnp.float32)

    def one_round(turn, carry):
        for hop in range(count):
            chunk = turn - hop
            live = (chunk >= 0) & (chunk < CHUNKS)
            if hop > 0:

                @pl.when(live & (me >= hop))
                def _():
                    copy(0, hop - 1, chunk, me - hop, me - 1).wait_recv()

                @pl.when(live & (me + hop < count))
                def _():
                    copy(1, hop - 1, chunk, me + hop, me + 1).wait_recv()

            if 0 < hop < count - 1:

                @pl.when(live & (me >= hop) & (me < count - 1))
                def _():
                    copy(0, hop, chunk, me - hop, me + 1).start()

                @pl.when(live & (me + hop < count) & (me > 0))
                def _():
                    copy(1, hop, chunk, me + hop, me - 1).start()

        send_own(turn + ahead, (turn + ahead) < CHUNKS)
        for index in range(3):

            @pl.when(turn == min(index, count - 2))
            def _():
                if index == 2:
                    sketch_copy.wait()
                build(index)

        base = turn - (count - 1)
        for o, owner in enumerate(owners):

            @pl.when((base >= 1) & (base <= CHUNKS) & (me != owner))
            def _():
                reduce_copy(o, base - 1, me).start()

            @pl.when((base >= SUMMED) & (base <= CHUNKS + SUMMED - 1) & (me == owner))
            def _():
                mine = rows_of(base - SUMMED, o)
                total = part_ref[mine, :].astype(jnp.float32)
                for sender in range(count):
                    if sender != owner:
                        reduce_copy(o, base - SUMMED, sender).wait_recv()
                        total = total + slots[sender, base - SUMMED].astype(jnp.float32)
                full_ref[mine, :] = total.astype(jnp.bfloat16)
                for target in range(count):
                    if target != owner:
                        spread_copy(o, base - SUMMED, target).start()

        @pl.when((base >= 0) & (base < CHUNKS))
        def _():
            here = pl.ds(pl.multiple_of(base * step, step), step)
            sum_ref[...] = jnp.zeros(sum_ref.shape, jnp.float32)
            low = jnp.concatenate([blocks[s, here, :] for s in range(count // 2)], axis=1)
            high = jnp.concatenate([blocks[s, here, :] for s in range(count // 2, count)], axis=1)
            full = jnp.concatenate([low, high], axis=1)

            def one_tile(j, unused):
                cols = pl.ds(pl.multiple_of(j * width, width), width)
                first = jnp.dot(low, sel_ref[:half, cols], preferred_element_type=jnp.float32)
                second = jnp.dot(low, sel_ref[half : 2 * half, cols], preferred_element_type=jnp.float32)
                third = jnp.dot(full, sel_ref[2 * half :, cols], preferred_element_type=jnp.float32)
                tile = (first * second * third).astype(jnp.bfloat16)
                tile_ref[here, cols] = tile
                sum_ref[...] += jnp.dot(tile, signs_ref[cols, :], preferred_element_type=jnp.float32)
                return unused

            lax.fori_loop(0, tiles, one_tile, 0, unroll=2)
            part_ref[here, :] = sum_ref[...].astype(jnp.bfloat16)

        for o, owner in enumerate(owners):

            @pl.when((base >= SPREAD) & (me != owner))
            def _():
                spread_copy(o, base - SPREAD, me).wait_recv()

        @pl.when(base >= SPREAD)
        def _():
            here = pl.ds(pl.multiple_of((base - SPREAD) * step, step), step)
            value = full_ref[here, :]
            turned = value.T
            gram_ref[...] += jnp.dot(turned, value, preferred_element_type=jnp.float32)

            def one_tile(j, unused):
                cols = pl.ds(pl.multiple_of(j * width, width), width)
                raw_ref[:, cols] += jnp.dot(turned, tile_ref[here, cols], preferred_element_type=jnp.float32)
                return unused

            lax.fori_loop(0, tiles, one_tile, 0)

        return carry

    lax.fori_loop(0, CHUNKS + count - 2 + SPREAD, one_round, 0)
    for o, owner in enumerate(owners):

        @pl.when(me != owner)
        def _():
            spread_copy(o, CHUNKS - 1, me).wait_recv()


    side = lax.rem(spot, 2)
    pairs = images // 2
    chips = [lax.rem(spot + 2 * k, images) for k in range(1, pairs)]
    span = feats // images
    rank_part = out_ref.shape[0]

    def columns(owner):
        return pl.ds(pl.multiple_of(owner * span, span), span)

    def remote(source, target, send, recv, device):
        return pltpu.make_async_remote_copy(
            src_ref=source, dst_ref=target, send_sem=send, recv_sem=recv, device_id={"img": device}, device_id_type=MESH
        )

    twin = spot + 1 - 2 * side
    mate = lax.div(spot, 2)
    order = [lax.rem(mate + k, pairs) for k in range(1, pairs + 1)]
    last = pl.ds((CHUNKS - 1) * step, step)
    value = full_ref[last, :]
    turned = value.T

    def raw_of(owner):
        return raw_ref[:, columns(owner)] + jnp.dot(
            turned, tile_ref[last, columns(owner)], preferred_element_type=jnp.float32
        )

    gram_ref[...] += jnp.dot(turned, value, preferred_element_type=jnp.float32)
    gram_pair = remote(gram_ref, pair_gram, gram_send.at[0], gram_recv.at[0], twin)
    gram_pair.start()
    pair_copies = []
    for k, m in enumerate(order):
        pair_staged[k] = raw_of(2 * m + 1 - side).astype(jnp.bfloat16)
        pair_copies.append(remote(pair_staged.at[k], pair_raw.at[k], pair_send.at[k], pair_recv.at[k], twin))
        pair_copies[-1].start()
    gram_pair.wait_recv()
    chip_gram[0] = gram_ref[...] + pair_gram[...]
    gram_copies = [
        remote(chip_gram.at[0], chip_gram.at[k + 1], gram_send.at[k + 1], gram_recv.at[k + 1], chip)
        for k, chip in enumerate(chips)
    ]
    for one in gram_copies:
        one.start()
    chip_copies = []
    for k, chip in enumerate(chips):
        both = raw_of(chip)
        pair_copies[k].wait_recv()
        chip_staged[k] = (both + pair_raw[k].astype(jnp.float32)).astype(jnp.bfloat16)
        chip_copies.append(remote(chip_staged.at[k], chip_raw.at[k], chip_send.at[k], chip_recv.at[k], chip))
        chip_copies[-1].start()
    mine = raw_of(spot)
    pair_copies[-1].wait_recv()
    mine = mine + pair_raw[pairs - 1].astype(jnp.float32)
    for one in gram_copies:
        one.wait_recv()
    total = jnp.zeros(gram_ref.shape, jnp.float32)
    for chip in range(pairs):
        total = total + chip_gram[lax.rem(lax.div(spot, 2) + pairs - chip, pairs)]
    factor_panels(scale, after, total, left, right, pivots, inverse_ref, min(PANEL, total.shape[0]))
    for k, one in enumerate(chip_copies):
        one.wait_recv()
        mine = mine + chip_raw[k].astype(jnp.float32)
    solved = jnp.dot(inverse_ref[...], mine, precision=lax.Precision.HIGHEST, preferred_element_type=jnp.float32) * root
    solved_ref[...] = solved.astype(jnp.bfloat16)

    def ranks(owner):
        return pl.ds(pl.multiple_of(owner * rank_part, rank_part), rank_part)

    row_copies = [
        remote(solved_ref.at[ranks(peer)], row_slots.at[k], row_send.at[k], row_recv.at[k], peer)
        for k, peer in enumerate(peers)
    ]
    for one in row_copies:
        one.start()
    value_ref[...] = full_ref[...]
    out_ref[:, columns(spot)] = solved_ref[ranks(spot), :].astype(jnp.float32)

    def drain(chunk, carry):
        for o, owner in enumerate(owners):

            @pl.when(me != owner)
            def _():
                reduce_copy(o, chunk, me).wait_send()

            @pl.when(me == owner)
            def _():
                for target in range(count):
                    if target != owner:
                        spread_copy(o, chunk, target).wait_send()

        for hop in range(count - 1):

            @pl.when((me >= hop) & (me < count - 1))
            def _():
                copy(0, hop, chunk, me - hop, me + 1).wait_send()

            @pl.when((me + hop < count) & (me > 0))
            def _():
                copy(1, hop, chunk, me + hop, me - 1).wait_send()

        return carry

    lax.fori_loop(0, CHUNKS, drain, 0)
    for k, one in enumerate(row_copies):
        one.wait_recv()
        out_ref[:, columns(lax.rem(spot + images - 1 - k, images))] = row_slots[k].astype(jnp.float32)
    for one in [gram_pair] + pair_copies + gram_copies + chip_copies + row_copies:
        one.wait_send()


def factor_and_project(coeffs, triples, sketch, count, images, scale, after, root):
    rows, part = coeffs.shape
    feats, rank = sketch.shape
    hops = max(count - 1, 1)
    step = rows // CHUNKS
    pairs = images // 2
    span = feats // images
    rank_part = rank // images
    square = pltpu.VMEM((rank, rank), jnp.float32)
    dma = pltpu.SemaphoreType.DMA
    return pl.pallas_call(
        functools.partial(whole_kernel, count, images, min(1024, feats), scale, after, root),
        in_specs=[HBM] * 3,
        out_specs=[VMEM] * 3,
        out_shape=[
            jax.ShapeDtypeStruct((rows, rank), jnp.bfloat16),
            jax.ShapeDtypeStruct((rank, rank), jnp.float32),
            jax.ShapeDtypeStruct((rank_part, feats), jnp.float32),
        ],
        scratch_shapes=[
            pltpu.VMEM(triples.shape, jnp.int32),
            pltpu.VMEM((feats, rank), jnp.int32),
            pltpu.VMEM((rows, feats), jnp.bfloat16),
            pltpu.VMEM((count, rows, part), jnp.bfloat16),
            pltpu.VMEM((2 * count * part, feats), jnp.bfloat16),
            pltpu.VMEM((feats, rank), jnp.bfloat16),
            pltpu.VMEM((step, rank), jnp.float32),
            pltpu.VMEM((rows, rank), jnp.bfloat16),
            pltpu.VMEM((count, CHUNKS, step // 2, rank), jnp.bfloat16),
            pltpu.VMEM((rows, rank), jnp.bfloat16),
            square,
            pltpu.VMEM((rank, feats), jnp.float32),
            square,
            pltpu.VMEM((pairs, rank, rank), jnp.float32),
            pltpu.VMEM((pairs, rank, span), jnp.bfloat16),
            pltpu.VMEM((pairs, rank, span), jnp.bfloat16),
            pltpu.VMEM((pairs - 1, rank, span), jnp.bfloat16),
            pltpu.VMEM((pairs - 1, rank, span), jnp.bfloat16),
            pltpu.VMEM((rank, span), jnp.bfloat16),
            pltpu.VMEM((images - 1, rank_part, span), jnp.bfloat16),
            square,
            square,
            square,
            dma((3,)),
            dma((2, hops, CHUNKS)),
            dma((2, hops, CHUNKS)),
            dma((2, CHUNKS)),
            dma((count, CHUNKS)),
            dma((count, CHUNKS)),
            dma((2, CHUNKS)),
        ]
        + [dma((pairs,))] * 4
        + [dma((pairs - 1,))] * 2
        + [dma((images - 1,))] * 2,
        compiler_params=pltpu.CompilerParams(
            collective_id=0, has_side_effects=True, vmem_limit_bytes=44 << 20
        ),
    )(*(pltpu.with_memory_space_constraint(array, pltpu.HBM) for array in (coeffs, triples, sketch)))


def on_device(coeffs, triples, sketch):
    rows_here = coeffs.shape[0]
    feats_here = triples.shape[1]
    img_count = lax.axis_size("img")
    feat_count = lax.axis_size("feat")
    total_rows = rows_here * img_count
    total_feats = feats_here * feat_count
    sketch_scale = (1.5 / total_feats) ** 0.5
    value, inverse, projected = factor_and_project(
        coeffs, triples, sketch, feat_count, img_count,
        sketch_scale * sketch_scale / total_rows, sketch_scale, total_rows**-0.5,
    )
    basis = jnp.dot(value.astype(jnp.float32), inverse.T, precision=lax.Precision.HIGHEST)
    return (basis, projected)


def solution(mesh):
    in_specs = (P("img", "feat"), P(None, "feat"), P("feat", None))
    out_specs = (P("img", None), P("img", "feat"))
    return jax.shard_map(
        on_device, mesh=mesh, in_specs=in_specs, out_specs=out_specs, check_vma=False
    )
```

```python
import functools

import jax
import jax.numpy as jnp
from jax import lax
from jax.experimental import pallas as pl
from jax.experimental.pallas import tpu as pltpu
from jax.sharding import PartitionSpec as P

CHUNKS = 8
AHEAD = (4, 1)
SUMMED = 5
SPREAD = 7
SUB = 8
PANEL = 32
PIECES = 4
MESH = pl.DeviceIdType.MESH
VMEM = pl.BlockSpec(memory_space=pltpu.VMEM)
HBM = pl.BlockSpec(memory_space=pltpu.HBM)


def greet(groups):
    barrier = pltpu.get_barrier_semaphore()
    for axis, peers in groups:
        for peer in peers:
            pl.semaphore_signal(barrier, inc=1, device_id={axis: peer}, device_id_type=MESH)
    pl.semaphore_wait(barrier, sum(len(peers) for axis, peers in groups))


def peers_of(me, count):
    return [lax.rem(me + k, count) for k in range(1, count)]


def factor_panels(scale, after, gram, left, right, pivots, out_ref, width):
    size = gram.shape[0]
    rows = lax.broadcasted_iota(jnp.int32, (width, size), 0)
    lanes = lax.broadcasted_iota(jnp.int32, (width, size), 1)
    left[...] = gram * scale
    whole_rows = lax.broadcasted_iota(jnp.int32, (size, size), 0)
    whole_lanes = lax.broadcasted_iota(jnp.int32, (size, size), 1)
    right[...] = jnp.where(whole_rows == whole_lanes, 1.0, 0.0)

    def panel(p, carry):
        first = pl.multiple_of(p * width, width)
        here = pl.ds(first, width)
        block = left[here, :]
        twin = right[here, :]
        inverse = jnp.zeros((width, size), jnp.float32)
        for start in range(0, width, SUB):
            columns = [
                jnp.take_along_axis(block, jnp.full((width, size), first + start + j, jnp.int32), axis=1)
                for j in range(SUB)
            ]
            for j in range(SUB):
                at = start + j
                ratio = 1.0 / columns[j][at : at + 1, :]
                inverse = jnp.where(rows == at, ratio, inverse)
                if at + 1 < width:
                    factor = jnp.where(rows > at, columns[j] * ratio, 0.0)
                    for m in range(j + 1, SUB):
                        columns[m] = columns[m] - factor * columns[m][at : at + 1, :]
                    block = block - factor * block[at : at + 1, :]
                    twin = twin - factor * twin[at : at + 1, :]
        pivots[here, :] = inverse
        right[here, :] = twin

        @pl.when(p + 1 < size // width)
        def _():
            factor = jnp.where(lanes >= first + width, block * inverse, 0.0)
            across = (((0,), (0,)), ((), ()))
            exact = lax.Precision.HIGHEST
            left[...] -= lax.dot_general(factor, block, across, precision=exact, preferred_element_type=jnp.float32)
            right[...] -= lax.dot_general(factor, twin, across, precision=exact, preferred_element_type=jnp.float32)

        return carry

    lax.fori_loop(0, size // width, panel, 0)
    out_ref[...] = right[...] * (after * jnp.sqrt(pivots[...]))


def whole_kernel(
    count, images, width, scale, after, root, coeffs_hbm, triples_hbm, sketch_hbm, basis_ref, out_ref,
    triples_ref, sketch_ref, tile_ref, blocks, sel_ref, signs_ref, sum_ref, part_ref, slots, full_ref, gram_ref,
    inverse_ref, raw_ref, pair_gram, chip_gram, pair_staged, pair_raw, chip_staged, chip_raw, solved_ref, row_slots, left, right,
    pivots, own_sem, send_sem, recv_sem, to_sem, from_sem, out_sem, in_sem, gram_send, gram_recv, pair_send, pair_recv,
    chip_send, chip_recv, row_send, row_recv
):
    me = lax.axis_index("feat")
    spot = lax.axis_index("img")
    rows, part = coeffs_hbm.shape
    feats = triples_ref.shape[1]
    step = rows // CHUNKS
    half = count * part // 2
    tiles = feats // width
    spans = ((0, half), (half, half), (2 * half, 2 * half))

    def build(index):
        start, depth = spans[index]

        def one(j, carry):
            cols = pl.ds(pl.multiple_of(j * width, width), width)
            levels = lax.broadcasted_iota(jnp.int32, (depth, width), 0)
            chosen = triples_ref[index : index + 1, cols]
            sel_ref[start : start + depth, cols] = jnp.where(levels == chosen, 1.0, 0.0).astype(jnp.bfloat16)
            if index == 2:
                signs_ref[cols, :] = sketch_ref[cols, :].astype(jnp.float32).astype(jnp.bfloat16)
            return carry

        lax.fori_loop(0, tiles, one, 0)

    own = pltpu.make_async_copy(coeffs_hbm, blocks.at[me], own_sem.at[0])
    own.start()
    triples_copy = pltpu.make_async_copy(triples_hbm, triples_ref, own_sem.at[1])
    triples_copy.start()
    sketch_copy = pltpu.make_async_copy(sketch_hbm, sketch_ref, own_sem.at[2])
    sketch_copy.start()
    peers = peers_of(spot, images)
    greet((("feat", peers_of(me, count)), ("img", peers)))
    own.wait()
    triples_copy.wait()

    def copy(side, hop, chunk, source, target):
        span = blocks.at[source, pl.ds(pl.multiple_of(chunk * step, step), step)]
        return pltpu.make_async_remote_copy(
            src_ref=span,
            dst_ref=span,
            send_sem=send_sem.at[side, hop, chunk],
            recv_sem=recv_sem.at[side, hop, chunk],
            device_id={"feat": target},
            device_id_type=MESH,
        )

    owners = (count // 2 - 1, count // 2)
    piece = step // len(owners)

    def rows_of(chunk, o):
        return pl.ds(pl.multiple_of(chunk * step + o * piece, piece), piece)

    def reduce_copy(o, chunk, sender):
        return pltpu.make_async_remote_copy(
            src_ref=part_ref.at[rows_of(chunk, o)],
            dst_ref=slots.at[sender, chunk],
            send_sem=to_sem.at[o, chunk],
            recv_sem=from_sem.at[sender, chunk],
            device_id={"feat": owners[o]},
            device_id_type=MESH,
        )

    def spread_copy(o, chunk, target):
        span = full_ref.at[rows_of(chunk, o)]
        return pltpu.make_async_remote_copy(
            src_ref=span,
            dst_ref=span,
            send_sem=out_sem.at[target, chunk],
            recv_sem=in_sem.at[o, chunk],
            device_id={"feat": target},
            device_id_type=MESH,
        )

    def send_own(chunk, live):
        @pl.when(live & (me < count - 1))
        def _():
            copy(0, 0, chunk, me, me + 1).start()

        @pl.when(live & (me > 0))
        def _():
            copy(1, 0, chunk, me, me - 1).start()

    ahead = AHEAD[0] + (AHEAD[1] - AHEAD[0]) * lax.rem(spot, 2)
    for chunk in range(max(AHEAD)):
        send_own(chunk, chunk < ahead)
    gram_ref[...] = jnp.zeros(gram_ref.shape, jnp.float32)
    raw_ref[...] = jnp.zeros(raw_ref.shape, jnp.float32)

    def one_round(turn, carry):
        for hop in range(count):
            chunk = turn - hop
            live = (chunk >= 0) & (chunk < CHUNKS)
            if hop > 0:

                @pl.when(live & (me >= hop))
                def _():
                    copy(0, hop - 1, chunk, me - hop, me - 1).wait_recv()

                @pl.when(live & (me + hop < count))
                def _():
                    copy(1, hop - 1, chunk, me + hop, me + 1).wait_recv()

            if 0 < hop < count - 1:

                @pl.when(live & (me >= hop) & (me < count - 1))
                def _():
                    copy(0, hop, chunk, me - hop, me + 1).start()

                @pl.when(live & (me + hop < count) & (me > 0))
                def _():
                    copy(1, hop, chunk, me + hop, me - 1).start()

        send_own(turn + ahead, (turn + ahead) < CHUNKS)
        for index in range(3):

            @pl.when(turn == min(index, count - 2))
            def _():
                if index == 2:
                    sketch_copy.wait()
                build(index)

        base = turn - (count - 1)
        for o, owner in enumerate(owners):

            @pl.when((base >= 1) & (base <= CHUNKS) & (me != owner))
            def _():
                reduce_copy(o, base - 1, me).start()

            @pl.when((base >= SUMMED) & (base <= CHUNKS + SUMMED - 1) & (me == owner))
            def _():
                mine = rows_of(base - SUMMED, o)
                total = part_ref[mine, :].astype(jnp.float32)
                for sender in range(count):
                    if sender != owner:
                        reduce_copy(o, base - SUMMED, sender).wait_recv()
                        total = total + slots[sender, base - SUMMED].astype(jnp.float32)
                full_ref[mine, :] = total.astype(jnp.bfloat16)
                for target in range(count):
                    if target != owner:
                        spread_copy(o, base - SUMMED, target).start()

        @pl.when((base >= 0) & (base < CHUNKS))
        def _():
            here = pl.ds(pl.multiple_of(base * step, step), step)
            sum_ref[...] = jnp.zeros(sum_ref.shape, jnp.float32)
            low = jnp.concatenate([blocks[s, here, :] for s in range(count // 2)], axis=1)
            high = jnp.concatenate([blocks[s, here, :] for s in range(count // 2, count)], axis=1)
            full = jnp.concatenate([low, high], axis=1)

            def one_tile(j, unused):
                cols = pl.ds(pl.multiple_of(j * width, width), width)
                first = jnp.dot(low, sel_ref[:half, cols], preferred_element_type=jnp.float32)
                second = jnp.dot(low, sel_ref[half : 2 * half, cols], preferred_element_type=jnp.float32)
                third = jnp.dot(full, sel_ref[2 * half :, cols], preferred_element_type=jnp.float32)
                tile = (first * second * third).astype(jnp.bfloat16)
                tile_ref[here, cols] = tile
                sum_ref[...] += jnp.dot(tile, signs_ref[cols, :], preferred_element_type=jnp.float32)
                return unused

            lax.fori_loop(0, tiles, one_tile, 0, unroll=2)
            part_ref[here, :] = sum_ref[...].astype(jnp.bfloat16)

        for o, owner in enumerate(owners):

            @pl.when((base >= SPREAD) & (me != owner))
            def _():
                spread_copy(o, base - SPREAD, me).wait_recv()

        @pl.when(base >= SPREAD)
        def _():
            here = pl.ds(pl.multiple_of((base - SPREAD) * step, step), step)
            value = full_ref[here, :]
            turned = value.T
            gram_ref[...] += jnp.dot(turned, value, preferred_element_type=jnp.float32)

            def one_tile(j, unused):
                cols = pl.ds(pl.multiple_of(j * width, width), width)
                raw_ref[:, cols] += jnp.dot(turned, tile_ref[here, cols], preferred_element_type=jnp.float32)
                return unused

            lax.fori_loop(0, tiles, one_tile, 0)

        return carry

    lax.fori_loop(0, CHUNKS + count - 2 + SPREAD, one_round, 0)
    for o, owner in enumerate(owners):

        @pl.when(me != owner)
        def _():
            spread_copy(o, CHUNKS - 1, me).wait_recv()


    side = lax.rem(spot, 2)
    pairs = images // 2
    chips = [lax.rem(spot + 2 * k, images) for k in range(1, pairs)]
    span = feats // images
    rank_part = out_ref.shape[0]

    def columns(owner):
        return pl.ds(pl.multiple_of(owner * span, span), span)

    def remote(source, target, send, recv, device):
        return pltpu.make_async_remote_copy(
            src_ref=source, dst_ref=target, send_sem=send, recv_sem=recv, device_id={"img": device}, device_id_type=MESH
        )

    twin = spot + 1 - 2 * side
    mate = lax.div(spot, 2)
    order = [lax.rem(mate + k, pairs) for k in range(1, pairs + 1)]
    last = pl.ds((CHUNKS - 1) * step, step)
    value = full_ref[last, :]
    turned = value.T

    def raw_of(owner):
        return raw_ref[:, columns(owner)] + jnp.dot(
            turned, tile_ref[last, columns(owner)], preferred_element_type=jnp.float32
        )

    gram_ref[...] += jnp.dot(turned, value, preferred_element_type=jnp.float32)
    gram_pair = remote(gram_ref, pair_gram, gram_send.at[0], gram_recv.at[0], twin)
    gram_pair.start()
    pair_copies = []
    for k, m in enumerate(order):
        pair_staged[k] = raw_of(2 * m + 1 - side).astype(jnp.bfloat16)
        pair_copies.append(remote(pair_staged.at[k], pair_raw.at[k], pair_send.at[k], pair_recv.at[k], twin))
        pair_copies[-1].start()
    gram_pair.wait_recv()
    chip_gram[0] = gram_ref[...] + pair_gram[...]
    gram_copies = [
        remote(chip_gram.at[0], chip_gram.at[k + 1], gram_send.at[k + 1], gram_recv.at[k + 1], chip)
        for k, chip in enumerate(chips)
    ]
    for one in gram_copies:
        one.start()
    chip_copies = []
    for k, chip in enumerate(chips):
        both = raw_of(chip)
        pair_copies[k].wait_recv()
        chip_staged[k] = (both + pair_raw[k].astype(jnp.float32)).astype(jnp.bfloat16)
        chip_copies.append(remote(chip_staged.at[k], chip_raw.at[k], chip_send.at[k], chip_recv.at[k], chip))
        chip_copies[-1].start()
    mine = raw_of(spot)
    pair_copies[-1].wait_recv()
    mine = mine + pair_raw[pairs - 1].astype(jnp.float32)
    for one in gram_copies:
        one.wait_recv()
    total = jnp.zeros(gram_ref.shape, jnp.float32)
    for chip in range(pairs):
        total = total + chip_gram[lax.rem(lax.div(spot, 2) + pairs - chip, pairs)]
    factor_panels(scale, after, total, left, right, pivots, inverse_ref, min(PANEL, total.shape[0]))
    for k, one in enumerate(chip_copies):
        one.wait_recv()
        mine = mine + chip_raw[k].astype(jnp.float32)
    solved = jnp.dot(inverse_ref[...], mine, precision=lax.Precision.HIGHEST, preferred_element_type=jnp.float32) * root
    solved_ref[...] = solved.astype(jnp.bfloat16)

    def ranks(owner):
        return pl.ds(pl.multiple_of(owner * rank_part, rank_part), rank_part)

    row_copies = [
        remote(solved_ref.at[ranks(peer)], row_slots.at[k], row_send.at[k], row_recv.at[k], peer)
        for k, peer in enumerate(peers)
    ]
    for one in row_copies:
        one.start()
    high = inverse_ref[...].astype(jnp.bfloat16)
    rest = inverse_ref[...] - high.astype(jnp.float32)
    middle = rest.astype(jnp.bfloat16)
    low = (rest - middle.astype(jnp.float32)).astype(jnp.bfloat16)
    turn_back = (((1,), (1,)), ((), ()))

    def one_block(j, carry):
        here = pl.ds(pl.multiple_of(j * step, step), step)
        block = full_ref[here, :]
        made = [
            lax.dot_general(block, piece, turn_back, preferred_element_type=jnp.float32) for piece in (low, middle, high)
        ]
        basis_ref[here, :] = made[0] + made[1] + made[2]
        return carry

    lax.fori_loop(0, CHUNKS, one_block, 0)
    out_ref[:, columns(spot)] = solved_ref[ranks(spot), :].astype(jnp.float32)

    def drain(chunk, carry):
        for o, owner in enumerate(owners):

            @pl.when(me != owner)
            def _():
                reduce_copy(o, chunk, me).wait_send()

            @pl.when(me == owner)
            def _():
                for target in range(count):
                    if target != owner:
                        spread_copy(o, chunk, target).wait_send()

        for hop in range(count - 1):

            @pl.when((me >= hop) & (me < count - 1))
            def _():
                copy(0, hop, chunk, me - hop, me + 1).wait_send()

            @pl.when((me + hop < count) & (me > 0))
            def _():
                copy(1, hop, chunk, me + hop, me - 1).wait_send()

        return carry

    lax.fori_loop(0, CHUNKS, drain, 0)
    for k, one in enumerate(row_copies):
        one.wait_recv()
        out_ref[:, columns(lax.rem(spot + images - 1 - k, images))] = row_slots[k].astype(jnp.float32)
    for one in [gram_pair] + pair_copies + gram_copies + chip_copies + row_copies:
        one.wait_send()


def factor_and_project(coeffs, triples, sketch, count, images, scale, after, root):
    rows, part = coeffs.shape
    feats, rank = sketch.shape
    hops = max(count - 1, 1)
    step = rows // CHUNKS
    pairs = images // 2
    span = feats // images
    rank_part = rank // images
    square = pltpu.VMEM((rank, rank), jnp.float32)
    dma = pltpu.SemaphoreType.DMA
    return pl.pallas_call(
        functools.partial(whole_kernel, count, images, min(1024, feats), scale, after, root),
        in_specs=[HBM] * 3,
        out_specs=[VMEM] * 2,
        out_shape=[
            jax.ShapeDtypeStruct((rows, rank), jnp.float32),
            jax.ShapeDtypeStruct((rank_part, feats), jnp.float32),
        ],
        scratch_shapes=[
            pltpu.VMEM(triples.shape, jnp.int32),
            pltpu.VMEM((feats, rank), jnp.int32),
            pltpu.VMEM((rows, feats), jnp.bfloat16),
            pltpu.VMEM((count, rows, part), jnp.bfloat16),
            pltpu.VMEM((2 * count * part, feats), jnp.bfloat16),
            pltpu.VMEM((feats, rank), jnp.bfloat16),
            pltpu.VMEM((step, rank), jnp.float32),
            pltpu.VMEM((rows, rank), jnp.bfloat16),
            pltpu.VMEM((count, CHUNKS, step // 2, rank), jnp.bfloat16),
            pltpu.VMEM((rows, rank), jnp.bfloat16),
            square,
            square,
            pltpu.VMEM((rank, feats), jnp.float32),
            square,
            pltpu.VMEM((pairs, rank, rank), jnp.float32),
            pltpu.VMEM((pairs, rank, span), jnp.bfloat16),
            pltpu.VMEM((pairs, rank, span), jnp.bfloat16),
            pltpu.VMEM((pairs - 1, rank, span), jnp.bfloat16),
            pltpu.VMEM((pairs - 1, rank, span), jnp.bfloat16),
            pltpu.VMEM((rank, span), jnp.bfloat16),
            pltpu.VMEM((images - 1, rank_part, span), jnp.bfloat16),
            square,
            square,
            square,
            dma((3,)),
            dma((2, hops, CHUNKS)),
            dma((2, hops, CHUNKS)),
            dma((2, CHUNKS)),
            dma((count, CHUNKS)),
            dma((count, CHUNKS)),
            dma((2, CHUNKS)),
        ]
        + [dma((pairs,))] * 4
        + [dma((pairs - 1,))] * 2
        + [dma((images - 1,))] * 2,
        compiler_params=pltpu.CompilerParams(
            collective_id=0, has_side_effects=True, vmem_limit_bytes=44 << 20
        ),
    )(*(pltpu.with_memory_space_constraint(array, pltpu.HBM) for array in (coeffs, triples, sketch)))


def hand_out_kernel(basis_ref, part_ref, basis_hbm, part_hbm, sems):
    step = basis_ref.shape[0] // PIECES
    copies = [pltpu.make_async_copy(part_ref, part_hbm, sems.at[PIECES])]
    for k in range(PIECES):
        here = pl.ds(k * step, step)
        copies.append(pltpu.make_async_copy(basis_ref.at[here], basis_hbm.at[here], sems.at[k]))
    for one in copies:
        one.start()
    for one in copies:
        one.wait()


def hand_out(basis, part):
    return pl.pallas_call(
        hand_out_kernel,
        in_specs=[VMEM] * 2,
        out_specs=[HBM] * 2,
        out_shape=[jax.ShapeDtypeStruct(basis.shape, basis.dtype), jax.ShapeDtypeStruct(part.shape, part.dtype)],
        scratch_shapes=[pltpu.SemaphoreType.DMA((PIECES + 1,))],
        compiler_params=pltpu.CompilerParams(vmem_limit_bytes=4 << 20),
    )(basis, part)


def on_device(coeffs, triples, sketch):
    rows_here = coeffs.shape[0]
    feats_here = triples.shape[1]
    img_count = lax.axis_size("img")
    feat_count = lax.axis_size("feat")
    total_rows = rows_here * img_count
    total_feats = feats_here * feat_count
    sketch_scale = (1.5 / total_feats) ** 0.5
    return hand_out(*factor_and_project(
        coeffs, triples, sketch, feat_count, img_count,
        sketch_scale * sketch_scale / total_rows, sketch_scale, total_rows**-0.5,
    ))


def solution(mesh):
    in_specs = (P("img", "feat"), P(None, "feat"), P("feat", None))
    out_specs = (P("img", None), P("img", "feat"))
    return jax.shard_map(
        on_device, mesh=mesh, in_specs=in_specs, out_specs=out_specs, check_vma=False
    )
```

```python
import functools

import jax
import jax.numpy as jnp
from jax import lax
from jax.experimental import pallas as pl
from jax.experimental.pallas import tpu as pltpu
from jax.sharding import PartitionSpec as P

CHUNKS = 8
AHEAD = (4, 1)
SUMMED = 4
EARLY = 3
SUB = 8
PANEL = 32
PIECES = 4
MESH = pl.DeviceIdType.MESH
VMEM = pl.BlockSpec(memory_space=pltpu.VMEM)
HBM = pl.BlockSpec(memory_space=pltpu.HBM)


def greet(groups):
    barrier = pltpu.get_barrier_semaphore()
    for axis, peers in groups:
        for peer in peers:
            pl.semaphore_signal(barrier, inc=1, device_id={axis: peer}, device_id_type=MESH)
    pl.semaphore_wait(barrier, sum(len(peers) for axis, peers in groups))


def peers_of(me, count):
    return [lax.rem(me + k, count) for k in range(1, count)]


def factor_panels(scale, after, gram, left, right, pivots, out_ref, width):
    size = gram.shape[0]
    rows = lax.broadcasted_iota(jnp.int32, (width, size), 0)
    lanes = lax.broadcasted_iota(jnp.int32, (width, size), 1)
    left[...] = gram * scale
    whole_rows = lax.broadcasted_iota(jnp.int32, (size, size), 0)
    whole_lanes = lax.broadcasted_iota(jnp.int32, (size, size), 1)
    right[...] = jnp.where(whole_rows == whole_lanes, 1.0, 0.0)

    def panel(p, carry):
        first = pl.multiple_of(p * width, width)
        here = pl.ds(first, width)
        block = left[here, :]
        twin = right[here, :]
        inverse = jnp.zeros((width, size), jnp.float32)
        for start in range(0, width, SUB):
            columns = [
                jnp.take_along_axis(block, jnp.full((width, size), first + start + j, jnp.int32), axis=1)
                for j in range(SUB)
            ]
            for j in range(SUB):
                at = start + j
                ratio = 1.0 / columns[j][at : at + 1, :]
                inverse = jnp.where(rows == at, ratio, inverse)
                if at + 1 < width:
                    factor = jnp.where(rows > at, columns[j] * ratio, 0.0)
                    for m in range(j + 1, SUB):
                        columns[m] = columns[m] - factor * columns[m][at : at + 1, :]
                    block = block - factor * block[at : at + 1, :]
                    twin = twin - factor * twin[at : at + 1, :]
        pivots[here, :] = inverse
        right[here, :] = twin

        @pl.when(p + 1 < size // width)
        def _():
            factor = jnp.where(lanes >= first + width, block * inverse, 0.0)
            across = (((0,), (0,)), ((), ()))
            exact = lax.Precision.HIGHEST
            left[...] -= lax.dot_general(factor, block, across, precision=exact, preferred_element_type=jnp.float32)
            right[...] -= lax.dot_general(factor, twin, across, precision=exact, preferred_element_type=jnp.float32)

        return carry

    lax.fori_loop(0, size // width, panel, 0)
    out_ref[...] = right[...] * (after * jnp.sqrt(pivots[...]))


def whole_kernel(
    count, images, width, scale, after, root, coeffs_hbm, triples_hbm, sketch_hbm, basis_ref, out_ref,
    triples_ref, sketch_ref, tile_ref, blocks, sel_ref, signs_ref, sum_ref, part_ref, slots, full_ref, gram_ref,
    inverse_ref, raw_ref, pair_gram, chip_gram, pair_staged, pair_raw, chip_staged, chip_raw, solved_ref, row_slots, left, right,
    pivots, own_sem, send_sem, recv_sem, to_sem, from_sem, out_sem, in_sem, gram_send, gram_recv, pair_send, pair_recv,
    chip_send, chip_recv, row_send, row_recv
):
    me = lax.axis_index("feat")
    spot = lax.axis_index("img")
    rows, part = coeffs_hbm.shape
    feats = triples_ref.shape[1]
    step = rows // CHUNKS
    half = count * part // 2
    tiles = feats // width
    spans = ((0, half), (half, half), (2 * half, 2 * half))

    def build(index):
        start, depth = spans[index]

        def one(j, carry):
            cols = pl.ds(pl.multiple_of(j * width, width), width)
            levels = lax.broadcasted_iota(jnp.int32, (depth, width), 0)
            chosen = triples_ref[index : index + 1, cols]
            sel_ref[start : start + depth, cols] = jnp.where(levels == chosen, 1.0, 0.0).astype(jnp.bfloat16)
            if index == 2:
                signs_ref[cols, :] = sketch_ref[cols, :].astype(jnp.float32).astype(jnp.bfloat16)
            return carry

        lax.fori_loop(0, tiles, one, 0)

    own = pltpu.make_async_copy(coeffs_hbm, blocks.at[me], own_sem.at[0])
    own.start()
    triples_copy = pltpu.make_async_copy(triples_hbm, triples_ref, own_sem.at[1])
    triples_copy.start()
    sketch_copy = pltpu.make_async_copy(sketch_hbm, sketch_ref, own_sem.at[2])
    sketch_copy.start()
    peers = peers_of(spot, images)
    greet((("feat", peers_of(me, count)), ("img", peers)))
    own.wait()
    triples_copy.wait()

    def copy(side, hop, chunk, source, target):
        span = blocks.at[source, pl.ds(pl.multiple_of(chunk * step, step), step)]
        return pltpu.make_async_remote_copy(
            src_ref=span,
            dst_ref=span,
            send_sem=send_sem.at[side, hop, chunk],
            recv_sem=recv_sem.at[side, hop, chunk],
            device_id={"feat": target},
            device_id_type=MESH,
        )

    owners = (count // 2 - 1, count // 2)
    piece = step // len(owners)

    def rows_of(chunk, o):
        return pl.ds(pl.multiple_of(chunk * step + o * piece, piece), piece)

    def reduce_copy(o, chunk, sender):
        return pltpu.make_async_remote_copy(
            src_ref=part_ref.at[rows_of(chunk, o)],
            dst_ref=slots.at[sender, chunk],
            send_sem=to_sem.at[o, chunk],
            recv_sem=from_sem.at[sender, chunk],
            device_id={"feat": owners[o]},
            device_id_type=MESH,
        )

    def spread_copy(o, chunk, target):
        span = full_ref.at[rows_of(chunk, o)]
        return pltpu.make_async_remote_copy(
            src_ref=span,
            dst_ref=span,
            send_sem=out_sem.at[target, chunk],
            recv_sem=in_sem.at[o, chunk],
            device_id={"feat": target},
            device_id_type=MESH,
        )

    def send_own(chunk, live):
        @pl.when(live & (me < count - 1))
        def _():
            copy(0, 0, chunk, me, me + 1).start()

        @pl.when(live & (me > 0))
        def _():
            copy(1, 0, chunk, me, me - 1).start()

    ahead = AHEAD[0] + (AHEAD[1] - AHEAD[0]) * lax.rem(spot, 2)
    for chunk in range(max(AHEAD)):
        send_own(chunk, chunk < ahead)

    def arrive(chunk):
        for o, owner in enumerate(owners):

            @pl.when(me != owner)
            def _():
                spread_copy(o, chunk, me).wait_recv()

    def add_up(start, stop):
        for chunk in range(start, stop):
            arrive(chunk)
        here = pl.ds(start * step, (stop - start) * step)
        value = full_ref[here, :]
        turned = value.T
        gram = jnp.dot(turned, value, preferred_element_type=jnp.float32)
        gram_ref[...] = gram if start == 0 else gram_ref[...] + gram

        def one_tile(j, unused):
            cols = pl.ds(pl.multiple_of(j * width, width), width)
            raw = jnp.dot(turned, tile_ref[here, cols], preferred_element_type=jnp.float32)
            raw_ref[:, cols] = raw if start == 0 else raw_ref[:, cols] + raw
            return unused

        lax.fori_loop(0, tiles, one_tile, 0)

    def one_round(turn, carry):
        for hop in range(count):
            chunk = turn - hop
            live = (chunk >= 0) & (chunk < CHUNKS)
            if hop > 0:

                @pl.when(live & (me >= hop))
                def _():
                    copy(0, hop - 1, chunk, me - hop, me - 1).wait_recv()

                @pl.when(live & (me + hop < count))
                def _():
                    copy(1, hop - 1, chunk, me + hop, me + 1).wait_recv()

            if 0 < hop < count - 1:

                @pl.when(live & (me >= hop) & (me < count - 1))
                def _():
                    copy(0, hop, chunk, me - hop, me + 1).start()

                @pl.when(live & (me + hop < count) & (me > 0))
                def _():
                    copy(1, hop, chunk, me + hop, me - 1).start()

        send_own(turn + ahead, (turn + ahead) < CHUNKS)
        for index in range(3):

            @pl.when(turn == min(index, count - 2))
            def _():
                if index == 2:
                    sketch_copy.wait()
                build(index)

        base = turn - (count - 1)
        for o, owner in enumerate(owners):

            @pl.when((base >= 1) & (base <= CHUNKS) & (me != owner))
            def _():
                reduce_copy(o, base - 1, me).start()

            @pl.when((base >= SUMMED) & (base <= CHUNKS + SUMMED - 1) & (me == owner))
            def _():
                mine = rows_of(base - SUMMED, o)
                total = part_ref[mine, :].astype(jnp.float32)
                for sender in range(count):
                    if sender != owner:
                        reduce_copy(o, base - SUMMED, sender).wait_recv()
                        total = total + slots[sender, base - SUMMED].astype(jnp.float32)
                full_ref[mine, :] = total.astype(jnp.bfloat16)
                for target in range(count):
                    if target != owner:
                        spread_copy(o, base - SUMMED, target).start()

        @pl.when((base >= 0) & (base < CHUNKS))
        def _():
            here = pl.ds(pl.multiple_of(base * step, step), step)
            sum_ref[...] = jnp.zeros(sum_ref.shape, jnp.float32)
            low = jnp.concatenate([blocks[s, here, :] for s in range(count // 2)], axis=1)
            high = jnp.concatenate([blocks[s, here, :] for s in range(count // 2, count)], axis=1)
            full = jnp.concatenate([low, high], axis=1)

            def one_tile(j, unused):
                cols = pl.ds(pl.multiple_of(j * width, width), width)
                first = jnp.dot(low, sel_ref[:half, cols], preferred_element_type=jnp.float32)
                second = jnp.dot(low, sel_ref[half : 2 * half, cols], preferred_element_type=jnp.float32)
                third = jnp.dot(full, sel_ref[2 * half :, cols], preferred_element_type=jnp.float32)
                tile = (first * second * third).astype(jnp.bfloat16)
                tile_ref[here, cols] = tile
                sum_ref[...] += jnp.dot(tile, signs_ref[cols, :], preferred_element_type=jnp.float32)
                return unused

            lax.fori_loop(0, tiles, one_tile, 0, unroll=2)
            part_ref[here, :] = sum_ref[...].astype(jnp.bfloat16)

        @pl.when(base == CHUNKS)
        def _():
            add_up(0, EARLY)

        return carry

    lax.fori_loop(0, CHUNKS + count - 1 + SUMMED, one_round, 0)
    add_up(EARLY, CHUNKS - 1)
    arrive(CHUNKS - 1)
    side = lax.rem(spot, 2)
    pairs = images // 2
    chips = [lax.rem(spot + 2 * k, images) for k in range(1, pairs)]
    span = feats // images
    rank_part = out_ref.shape[0]

    def columns(owner):
        return pl.ds(pl.multiple_of(owner * span, span), span)

    def remote(source, target, send, recv, device):
        return pltpu.make_async_remote_copy(
            src_ref=source, dst_ref=target, send_sem=send, recv_sem=recv, device_id={"img": device}, device_id_type=MESH
        )

    twin = spot + 1 - 2 * side
    mate = lax.div(spot, 2)
    order = [lax.rem(mate + k, pairs) for k in range(1, pairs + 1)]
    last = pl.ds((CHUNKS - 1) * step, step)
    value = full_ref[last, :]
    turned = value.T

    def raw_of(owner):
        return raw_ref[:, columns(owner)] + jnp.dot(
            turned, tile_ref[last, columns(owner)], preferred_element_type=jnp.float32
        )

    gram_ref[...] += jnp.dot(turned, value, preferred_element_type=jnp.float32)
    gram_pair = remote(gram_ref, pair_gram, gram_send.at[0], gram_recv.at[0], twin)
    gram_pair.start()
    pair_copies = []
    for k, m in enumerate(order):
        pair_staged[k] = raw_of(2 * m + 1 - side).astype(jnp.bfloat16)
        pair_copies.append(remote(pair_staged.at[k], pair_raw.at[k], pair_send.at[k], pair_recv.at[k], twin))
        pair_copies[-1].start()
    gram_pair.wait_recv()
    chip_gram[0] = gram_ref[...] + pair_gram[...]
    gram_copies = [
        remote(chip_gram.at[0], chip_gram.at[k + 1], gram_send.at[k + 1], gram_recv.at[k + 1], chip)
        for k, chip in enumerate(chips)
    ]
    for one in gram_copies:
        one.start()
    chip_copies = []
    for k, chip in enumerate(chips):
        both = raw_of(chip)
        pair_copies[k].wait_recv()
        chip_staged[k] = (both + pair_raw[k].astype(jnp.float32)).astype(jnp.bfloat16)
        chip_copies.append(remote(chip_staged.at[k], chip_raw.at[k], chip_send.at[k], chip_recv.at[k], chip))
        chip_copies[-1].start()
    mine = raw_of(spot)
    pair_copies[-1].wait_recv()
    mine = mine + pair_raw[pairs - 1].astype(jnp.float32)
    for one in gram_copies:
        one.wait_recv()
    total = jnp.zeros(gram_ref.shape, jnp.float32)
    for chip in range(pairs):
        total = total + chip_gram[lax.rem(lax.div(spot, 2) + pairs - chip, pairs)]
    factor_panels(scale, after, total, left, right, pivots, inverse_ref, min(PANEL, total.shape[0]))
    for k, one in enumerate(chip_copies):
        one.wait_recv()
        mine = mine + chip_raw[k].astype(jnp.float32)
    solved = jnp.dot(inverse_ref[...], mine, precision=lax.Precision.HIGHEST, preferred_element_type=jnp.float32) * root
    solved_ref[...] = solved.astype(jnp.bfloat16)

    def ranks(owner):
        return pl.ds(pl.multiple_of(owner * rank_part, rank_part), rank_part)

    row_copies = [
        remote(solved_ref.at[ranks(peer)], row_slots.at[k], row_send.at[k], row_recv.at[k], peer)
        for k, peer in enumerate(peers)
    ]
    for one in row_copies:
        one.start()
    high = inverse_ref[...].astype(jnp.bfloat16)
    rest = inverse_ref[...] - high.astype(jnp.float32)
    middle = rest.astype(jnp.bfloat16)
    low = (rest - middle.astype(jnp.float32)).astype(jnp.bfloat16)
    turn_back = (((1,), (1,)), ((), ()))

    def one_block(j, carry):
        here = pl.ds(pl.multiple_of(j * step, step), step)
        block = full_ref[here, :]
        made = [
            lax.dot_general(block, piece, turn_back, preferred_element_type=jnp.float32) for piece in (low, middle, high)
        ]
        basis_ref[here, :] = made[0] + made[1] + made[2]
        return carry

    lax.fori_loop(0, CHUNKS, one_block, 0)
    out_ref[:, columns(spot)] = solved_ref[ranks(spot), :].astype(jnp.float32)

    def drain(chunk, carry):
        for o, owner in enumerate(owners):

            @pl.when(me != owner)
            def _():
                reduce_copy(o, chunk, me).wait_send()

            @pl.when(me == owner)
            def _():
                for target in range(count):
                    if target != owner:
                        spread_copy(o, chunk, target).wait_send()

        for hop in range(count - 1):

            @pl.when((me >= hop) & (me < count - 1))
            def _():
                copy(0, hop, chunk, me - hop, me + 1).wait_send()

            @pl.when((me + hop < count) & (me > 0))
            def _():
                copy(1, hop, chunk, me + hop, me - 1).wait_send()

        return carry

    lax.fori_loop(0, CHUNKS, drain, 0)
    for k, one in enumerate(row_copies):
        one.wait_recv()
        out_ref[:, columns(lax.rem(spot + images - 1 - k, images))] = row_slots[k].astype(jnp.float32)
    for one in [gram_pair] + pair_copies + gram_copies + chip_copies + row_copies:
        one.wait_send()


def factor_and_project(coeffs, triples, sketch, count, images, scale, after, root):
    rows, part = coeffs.shape
    feats, rank = sketch.shape
    hops = max(count - 1, 1)
    step = rows // CHUNKS
    pairs = images // 2
    span = feats // images
    rank_part = rank // images
    square = pltpu.VMEM((rank, rank), jnp.float32)
    dma = pltpu.SemaphoreType.DMA
    return pl.pallas_call(
        functools.partial(whole_kernel, count, images, min(1024, feats), scale, after, root),
        in_specs=[HBM] * 3,
        out_specs=[VMEM] * 2,
        out_shape=[
            jax.ShapeDtypeStruct((rows, rank), jnp.float32),
            jax.ShapeDtypeStruct((rank_part, feats), jnp.float32),
        ],
        scratch_shapes=[
            pltpu.VMEM(triples.shape, jnp.int32),
            pltpu.VMEM((feats, rank), jnp.int32),
            pltpu.VMEM((rows, feats), jnp.bfloat16),
            pltpu.VMEM((count, rows, part), jnp.bfloat16),
            pltpu.VMEM((2 * count * part, feats), jnp.bfloat16),
            pltpu.VMEM((feats, rank), jnp.bfloat16),
            pltpu.VMEM((step, rank), jnp.float32),
            pltpu.VMEM((rows, rank), jnp.bfloat16),
            pltpu.VMEM((count, CHUNKS, step // 2, rank), jnp.bfloat16),
            pltpu.VMEM((rows, rank), jnp.bfloat16),
            square,
            square,
            pltpu.VMEM((rank, feats), jnp.float32),
            square,
            pltpu.VMEM((pairs, rank, rank), jnp.float32),
            pltpu.VMEM((pairs, rank, span), jnp.bfloat16),
            pltpu.VMEM((pairs, rank, span), jnp.bfloat16),
            pltpu.VMEM((pairs - 1, rank, span), jnp.bfloat16),
            pltpu.VMEM((pairs - 1, rank, span), jnp.bfloat16),
            pltpu.VMEM((rank, span), jnp.bfloat16),
            pltpu.VMEM((images - 1, rank_part, span), jnp.bfloat16),
            square,
            square,
            square,
            dma((3,)),
            dma((2, hops, CHUNKS)),
            dma((2, hops, CHUNKS)),
            dma((2, CHUNKS)),
            dma((count, CHUNKS)),
            dma((count, CHUNKS)),
            dma((2, CHUNKS)),
        ]
        + [dma((pairs,))] * 4
        + [dma((pairs - 1,))] * 2
        + [dma((images - 1,))] * 2,
        compiler_params=pltpu.CompilerParams(
            collective_id=0, has_side_effects=True, vmem_limit_bytes=44 << 20
        ),
    )(*(pltpu.with_memory_space_constraint(array, pltpu.HBM) for array in (coeffs, triples, sketch)))


def hand_out_kernel(basis_ref, part_ref, basis_hbm, part_hbm, sems):
    step = basis_ref.shape[0] // PIECES
    copies = [pltpu.make_async_copy(part_ref, part_hbm, sems.at[PIECES])]
    for k in range(PIECES):
        here = pl.ds(k * step, step)
        copies.append(pltpu.make_async_copy(basis_ref.at[here], basis_hbm.at[here], sems.at[k]))
    for one in copies:
        one.start()
    for one in copies:
        one.wait()


def hand_out(basis, part):
    return pl.pallas_call(
        hand_out_kernel,
        in_specs=[VMEM] * 2,
        out_specs=[HBM] * 2,
        out_shape=[jax.ShapeDtypeStruct(basis.shape, basis.dtype), jax.ShapeDtypeStruct(part.shape, part.dtype)],
        scratch_shapes=[pltpu.SemaphoreType.DMA((PIECES + 1,))],
        compiler_params=pltpu.CompilerParams(vmem_limit_bytes=4 << 20),
    )(basis, part)


def on_device(coeffs, triples, sketch):
    rows_here = coeffs.shape[0]
    feats_here = triples.shape[1]
    img_count = lax.axis_size("img")
    feat_count = lax.axis_size("feat")
    total_rows = rows_here * img_count
    total_feats = feats_here * feat_count
    sketch_scale = (1.5 / total_feats) ** 0.5
    return hand_out(*factor_and_project(
        coeffs, triples, sketch, feat_count, img_count,
        sketch_scale * sketch_scale / total_rows, sketch_scale, total_rows**-0.5,
    ))


def solution(mesh):
    in_specs = (P("img", "feat"), P(None, "feat"), P("feat", None))
    out_specs = (P("img", None), P("img", "feat"))
    return jax.shard_map(
        on_device, mesh=mesh, in_specs=in_specs, out_specs=out_specs, check_vma=False
    )
```

```python
import functools

import jax
import jax.numpy as jnp
from jax import lax
from jax.experimental import pallas as pl
from jax.experimental.pallas import tpu as pltpu
from jax.sharding import PartitionSpec as P

CHUNKS = 8
AHEAD = (3, 1)
SUMMED = 4
EARLY = 3
SUB = 8
PANEL = 32
PIECES = 4
MESH = pl.DeviceIdType.MESH
VMEM = pl.BlockSpec(memory_space=pltpu.VMEM)
HBM = pl.BlockSpec(memory_space=pltpu.HBM)


def greet(groups):
    barrier = pltpu.get_barrier_semaphore()
    for axis, peers in groups:
        for peer in peers:
            pl.semaphore_signal(barrier, inc=1, device_id={axis: peer}, device_id_type=MESH)
    pl.semaphore_wait(barrier, sum(len(peers) for axis, peers in groups))


def peers_of(me, count):
    return [lax.rem(me + k, count) for k in range(1, count)]


def factor_panels(scale, after, gram, left, right, pivots, out_ref, width):
    size = gram.shape[0]
    rows = lax.broadcasted_iota(jnp.int32, (width, size), 0)
    lanes = lax.broadcasted_iota(jnp.int32, (width, size), 1)
    left[...] = gram * scale
    whole_rows = lax.broadcasted_iota(jnp.int32, (size, size), 0)
    whole_lanes = lax.broadcasted_iota(jnp.int32, (size, size), 1)
    right[...] = jnp.where(whole_rows == whole_lanes, 1.0, 0.0)

    def panel(p, carry):
        first = pl.multiple_of(p * width, width)
        here = pl.ds(first, width)
        block = left[here, :]
        twin = right[here, :]
        inverse = jnp.zeros((width, size), jnp.float32)
        for start in range(0, width, SUB):
            columns = [
                jnp.take_along_axis(block, jnp.full((width, size), first + start + j, jnp.int32), axis=1)
                for j in range(SUB)
            ]
            for j in range(SUB):
                at = start + j
                ratio = 1.0 / columns[j][at : at + 1, :]
                inverse = jnp.where(rows == at, ratio, inverse)
                if at + 1 < width:
                    factor = jnp.where(rows > at, columns[j] * ratio, 0.0)
                    for m in range(j + 1, SUB):
                        columns[m] = columns[m] - factor * columns[m][at : at + 1, :]
                    block = block - factor * block[at : at + 1, :]
                    twin = twin - factor * twin[at : at + 1, :]
        pivots[here, :] = inverse
        right[here, :] = twin

        @pl.when(p + 1 < size // width)
        def _():
            factor = jnp.where(lanes >= first + width, block * inverse, 0.0)
            across = (((0,), (0,)), ((), ()))
            exact = lax.Precision.HIGHEST
            left[...] -= lax.dot_general(factor, block, across, precision=exact, preferred_element_type=jnp.float32)
            right[...] -= lax.dot_general(factor, twin, across, precision=exact, preferred_element_type=jnp.float32)

        return carry

    lax.fori_loop(0, size // width, panel, 0)
    out_ref[...] = right[...] * (after * jnp.sqrt(pivots[...]))


def whole_kernel(
    count, images, width, scale, after, root, coeffs_hbm, triples_hbm, sketch_hbm, basis_ref, out_ref,
    triples_ref, sketch_ref, tile_ref, blocks, sel_ref, signs_ref, sum_ref, part_ref, slots, full_ref, gram_ref,
    inverse_ref, raw_ref, pair_gram, chip_gram, pair_staged, pair_raw, chip_staged, chip_raw, solved_ref, row_slots, left, right,
    pivots, own_sem, send_sem, recv_sem, to_sem, from_sem, out_sem, in_sem, gram_send, gram_recv, pair_send, pair_recv,
    chip_send, chip_recv, row_send, row_recv
):
    me = lax.axis_index("feat")
    spot = lax.axis_index("img")
    rows, part = coeffs_hbm.shape
    feats = triples_ref.shape[1]
    step = rows // CHUNKS
    half = count * part // 2
    tiles = feats // width
    spans = ((0, half), (half, half), (2 * half, 2 * half))

    def build(index):
        start, depth = spans[index]

        def one(j, carry):
            cols = pl.ds(pl.multiple_of(j * width, width), width)
            levels = lax.broadcasted_iota(jnp.int32, (depth, width), 0)
            chosen = triples_ref[index : index + 1, cols]
            sel_ref[start : start + depth, cols] = jnp.where(levels == chosen, 1.0, 0.0).astype(jnp.bfloat16)
            if index == 2:
                signs_ref[cols, :] = sketch_ref[cols, :].astype(jnp.float32).astype(jnp.bfloat16)
            return carry

        lax.fori_loop(0, tiles, one, 0)

    own = pltpu.make_async_copy(coeffs_hbm, blocks.at[me], own_sem.at[0])
    own.start()
    triples_copy = pltpu.make_async_copy(triples_hbm, triples_ref, own_sem.at[1])
    triples_copy.start()
    sketch_copy = pltpu.make_async_copy(sketch_hbm, sketch_ref, own_sem.at[2])
    sketch_copy.start()
    peers = peers_of(spot, images)
    greet((("feat", peers_of(me, count)), ("img", peers)))
    own.wait()
    triples_copy.wait()

    def copy(side, hop, chunk, source, target):
        span = blocks.at[source, pl.ds(pl.multiple_of(chunk * step, step), step)]
        return pltpu.make_async_remote_copy(
            src_ref=span,
            dst_ref=span,
            send_sem=send_sem.at[side, hop, chunk],
            recv_sem=recv_sem.at[side, hop, chunk],
            device_id={"feat": target},
            device_id_type=MESH,
        )

    owners = (count // 2 - 1, count // 2)
    piece = step // len(owners)

    def rows_of(chunk, o):
        return pl.ds(pl.multiple_of(chunk * step + o * piece, piece), piece)

    def reduce_copy(o, chunk, sender):
        return pltpu.make_async_remote_copy(
            src_ref=part_ref.at[rows_of(chunk, o)],
            dst_ref=slots.at[sender, chunk],
            send_sem=to_sem.at[o, chunk],
            recv_sem=from_sem.at[sender, chunk],
            device_id={"feat": owners[o]},
            device_id_type=MESH,
        )

    def spread_copy(o, chunk, target):
        span = full_ref.at[rows_of(chunk, o)]
        return pltpu.make_async_remote_copy(
            src_ref=span,
            dst_ref=span,
            send_sem=out_sem.at[target, chunk],
            recv_sem=in_sem.at[o, chunk],
            device_id={"feat": target},
            device_id_type=MESH,
        )

    def send_own(chunk, live):
        @pl.when(live & (me < count - 1))
        def _():
            copy(0, 0, chunk, me, me + 1).start()

        @pl.when(live & (me > 0))
        def _():
            copy(1, 0, chunk, me, me - 1).start()

    ahead = AHEAD[0] + (AHEAD[1] - AHEAD[0]) * lax.rem(spot, 2)
    for chunk in range(max(AHEAD)):
        send_own(chunk, chunk < ahead)

    def arrive(chunk):
        for o, owner in enumerate(owners):

            @pl.when(me != owner)
            def _():
                spread_copy(o, chunk, me).wait_recv()

    def add_up(start, stop):
        for chunk in range(start, stop):
            arrive(chunk)
        here = pl.ds(start * step, (stop - start) * step)
        value = full_ref[here, :]
        turned = value.T
        gram = jnp.dot(turned, value, preferred_element_type=jnp.float32)
        gram_ref[...] = gram if start == 0 else gram_ref[...] + gram

        def one_tile(j, unused):
            cols = pl.ds(pl.multiple_of(j * width, width), width)
            raw = jnp.dot(turned, tile_ref[here, cols], preferred_element_type=jnp.float32)
            raw_ref[:, cols] = raw if start == 0 else raw_ref[:, cols] + raw
            return unused

        lax.fori_loop(0, tiles, one_tile, 0)

    def one_round(turn, carry):
        for hop in range(count):
            chunk = turn - hop
            live = (chunk >= 0) & (chunk < CHUNKS)
            if hop > 0:

                @pl.when(live & (me >= hop))
                def _():
                    copy(0, hop - 1, chunk, me - hop, me - 1).wait_recv()

                @pl.when(live & (me + hop < count))
                def _():
                    copy(1, hop - 1, chunk, me + hop, me + 1).wait_recv()

            if 0 < hop < count - 1:

                @pl.when(live & (me >= hop) & (me < count - 1))
                def _():
                    copy(0, hop, chunk, me - hop, me + 1).start()

                @pl.when(live & (me + hop < count) & (me > 0))
                def _():
                    copy(1, hop, chunk, me + hop, me - 1).start()

        send_own(turn + ahead, (turn + ahead) < CHUNKS)
        for index in range(3):

            @pl.when(turn == min(index, count - 2))
            def _():
                if index == 2:
                    sketch_copy.wait()
                build(index)

        base = turn - (count - 1)
        for o, owner in enumerate(owners):

            @pl.when((base >= 1) & (base <= CHUNKS) & (me != owner))
            def _():
                reduce_copy(o, base - 1, me).start()

            @pl.when((base >= SUMMED) & (base <= CHUNKS + SUMMED - 1) & (me == owner))
            def _():
                mine = rows_of(base - SUMMED, o)
                total = part_ref[mine, :].astype(jnp.float32)
                for sender in range(count):
                    if sender != owner:
                        reduce_copy(o, base - SUMMED, sender).wait_recv()
                        total = total + slots[sender, base - SUMMED].astype(jnp.float32)
                full_ref[mine, :] = total.astype(jnp.bfloat16)
                for target in range(count):
                    if target != owner:
                        spread_copy(o, base - SUMMED, target).start()

        @pl.when((base >= 0) & (base < CHUNKS))
        def _():
            here = pl.ds(pl.multiple_of(base * step, step), step)
            sum_ref[...] = jnp.zeros(sum_ref.shape, jnp.float32)
            low = jnp.concatenate([blocks[s, here, :] for s in range(count // 2)], axis=1)
            high = jnp.concatenate([blocks[s, here, :] for s in range(count // 2, count)], axis=1)
            full = jnp.concatenate([low, high], axis=1)

            def one_tile(j, unused):
                cols = pl.ds(pl.multiple_of(j * width, width), width)
                first = jnp.dot(low, sel_ref[:half, cols], preferred_element_type=jnp.float32)
                second = jnp.dot(low, sel_ref[half : 2 * half, cols], preferred_element_type=jnp.float32)
                third = jnp.dot(full, sel_ref[2 * half :, cols], preferred_element_type=jnp.float32)
                tile = (first * second * third).astype(jnp.bfloat16)
                tile_ref[here, cols] = tile
                sum_ref[...] += jnp.dot(tile, signs_ref[cols, :], preferred_element_type=jnp.float32)
                return unused

            lax.fori_loop(0, tiles, one_tile, 0, unroll=4)
            part_ref[here, :] = sum_ref[...].astype(jnp.bfloat16)

        @pl.when(base == CHUNKS)
        def _():
            add_up(0, EARLY)

        return carry

    lax.fori_loop(0, CHUNKS + count - 1 + SUMMED, one_round, 0)
    add_up(EARLY, CHUNKS - 1)
    arrive(CHUNKS - 1)
    side = lax.rem(spot, 2)
    pairs = images // 2
    chips = [lax.rem(spot + 2 * k, images) for k in range(1, pairs)]
    span = feats // images
    rank_part = out_ref.shape[0]

    def columns(owner):
        return pl.ds(pl.multiple_of(owner * span, span), span)

    def remote(source, target, send, recv, device):
        return pltpu.make_async_remote_copy(
            src_ref=source, dst_ref=target, send_sem=send, recv_sem=recv, device_id={"img": device}, device_id_type=MESH
        )

    twin = spot + 1 - 2 * side
    mate = lax.div(spot, 2)
    order = [lax.rem(mate + k, pairs) for k in range(1, pairs + 1)]
    last = pl.ds((CHUNKS - 1) * step, step)
    value = full_ref[last, :]
    turned = value.T

    def raw_of(owner):
        return raw_ref[:, columns(owner)] + jnp.dot(
            turned, tile_ref[last, columns(owner)], preferred_element_type=jnp.float32
        )

    gram_ref[...] += jnp.dot(turned, value, preferred_element_type=jnp.float32)
    gram_pair = remote(gram_ref, pair_gram, gram_send.at[0], gram_recv.at[0], twin)
    gram_pair.start()
    pair_copies = []
    for k, m in enumerate(order):
        pair_staged[k] = raw_of(2 * m + 1 - side).astype(jnp.bfloat16)
        pair_copies.append(remote(pair_staged.at[k], pair_raw.at[k], pair_send.at[k], pair_recv.at[k], twin))
        pair_copies[-1].start()
    gram_pair.wait_recv()
    chip_gram[0] = gram_ref[...] + pair_gram[...]
    gram_copies = [
        remote(chip_gram.at[0], chip_gram.at[k + 1], gram_send.at[k + 1], gram_recv.at[k + 1], chip)
        for k, chip in enumerate(chips)
    ]
    for one in gram_copies:
        one.start()
    chip_copies = []
    for k, chip in enumerate(chips):
        both = raw_of(chip)
        pair_copies[k].wait_recv()
        chip_staged[k] = (both + pair_raw[k].astype(jnp.float32)).astype(jnp.bfloat16)
        chip_copies.append(remote(chip_staged.at[k], chip_raw.at[k], chip_send.at[k], chip_recv.at[k], chip))
        chip_copies[-1].start()
    mine = raw_of(spot)
    pair_copies[-1].wait_recv()
    mine = mine + pair_raw[pairs - 1].astype(jnp.float32)
    for one in gram_copies:
        one.wait_recv()
    total = jnp.zeros(gram_ref.shape, jnp.float32)
    for chip in range(pairs):
        total = total + chip_gram[lax.rem(lax.div(spot, 2) + pairs - chip, pairs)]
    factor_panels(scale, after, total, left, right, pivots, inverse_ref, min(PANEL, total.shape[0]))
    for k, one in enumerate(chip_copies):
        one.wait_recv()
        mine = mine + chip_raw[k].astype(jnp.float32)
    solved = jnp.dot(inverse_ref[...], mine, precision=lax.Precision.HIGHEST, preferred_element_type=jnp.float32) * root
    solved_ref[...] = solved.astype(jnp.bfloat16)

    def ranks(owner):
        return pl.ds(pl.multiple_of(owner * rank_part, rank_part), rank_part)

    row_copies = [
        remote(solved_ref.at[ranks(peer)], row_slots.at[k], row_send.at[k], row_recv.at[k], peer)
        for k, peer in enumerate(peers)
    ]
    for one in row_copies:
        one.start()
    high = inverse_ref[...].astype(jnp.bfloat16)
    rest = inverse_ref[...] - high.astype(jnp.float32)
    middle = rest.astype(jnp.bfloat16)
    low = (rest - middle.astype(jnp.float32)).astype(jnp.bfloat16)
    turn_back = (((1,), (1,)), ((), ()))

    def one_block(j, carry):
        here = pl.ds(pl.multiple_of(j * step, step), step)
        block = full_ref[here, :]
        made = [
            lax.dot_general(block, piece, turn_back, preferred_element_type=jnp.float32) for piece in (low, middle, high)
        ]
        basis_ref[here, :] = made[0] + made[1] + made[2]
        return carry

    lax.fori_loop(0, CHUNKS, one_block, 0)
    out_ref[:, columns(spot)] = solved_ref[ranks(spot), :].astype(jnp.float32)

    def drain(chunk, carry):
        for o, owner in enumerate(owners):

            @pl.when(me != owner)
            def _():
                reduce_copy(o, chunk, me).wait_send()

            @pl.when(me == owner)
            def _():
                for target in range(count):
                    if target != owner:
                        spread_copy(o, chunk, target).wait_send()

        for hop in range(count - 1):

            @pl.when((me >= hop) & (me < count - 1))
            def _():
                copy(0, hop, chunk, me - hop, me + 1).wait_send()

            @pl.when((me + hop < count) & (me > 0))
            def _():
                copy(1, hop, chunk, me + hop, me - 1).wait_send()

        return carry

    lax.fori_loop(0, CHUNKS, drain, 0)
    for k, one in enumerate(row_copies):
        one.wait_recv()
        out_ref[:, columns(lax.rem(spot + images - 1 - k, images))] = row_slots[k].astype(jnp.float32)
    for one in [gram_pair] + pair_copies + gram_copies + chip_copies + row_copies:
        one.wait_send()


def factor_and_project(coeffs, triples, sketch, count, images, scale, after, root):
    rows, part = coeffs.shape
    feats, rank = sketch.shape
    hops = max(count - 1, 1)
    step = rows // CHUNKS
    pairs = images // 2
    span = feats // images
    rank_part = rank // images
    square = pltpu.VMEM((rank, rank), jnp.float32)
    dma = pltpu.SemaphoreType.DMA
    return pl.pallas_call(
        functools.partial(whole_kernel, count, images, min(1024, feats), scale, after, root),
        in_specs=[HBM] * 3,
        out_specs=[VMEM] * 2,
        out_shape=[
            jax.ShapeDtypeStruct((rows, rank), jnp.float32),
            jax.ShapeDtypeStruct((rank_part, feats), jnp.float32),
        ],
        scratch_shapes=[
            pltpu.VMEM(triples.shape, jnp.int32),
            pltpu.VMEM((feats, rank), jnp.int32),
            pltpu.VMEM((rows, feats), jnp.bfloat16),
            pltpu.VMEM((count, rows, part), jnp.bfloat16),
            pltpu.VMEM((2 * count * part, feats), jnp.bfloat16),
            pltpu.VMEM((feats, rank), jnp.bfloat16),
            pltpu.VMEM((step, rank), jnp.float32),
            pltpu.VMEM((rows, rank), jnp.bfloat16),
            pltpu.VMEM((count, CHUNKS, step // 2, rank), jnp.bfloat16),
            pltpu.VMEM((rows, rank), jnp.bfloat16),
            square,
            square,
            pltpu.VMEM((rank, feats), jnp.float32),
            square,
            pltpu.VMEM((pairs, rank, rank), jnp.float32),
            pltpu.VMEM((pairs, rank, span), jnp.bfloat16),
            pltpu.VMEM((pairs, rank, span), jnp.bfloat16),
            pltpu.VMEM((pairs - 1, rank, span), jnp.bfloat16),
            pltpu.VMEM((pairs - 1, rank, span), jnp.bfloat16),
            pltpu.VMEM((rank, span), jnp.bfloat16),
            pltpu.VMEM((images - 1, rank_part, span), jnp.bfloat16),
            square,
            square,
            square,
            dma((3,)),
            dma((2, hops, CHUNKS)),
            dma((2, hops, CHUNKS)),
            dma((2, CHUNKS)),
            dma((count, CHUNKS)),
            dma((count, CHUNKS)),
            dma((2, CHUNKS)),
        ]
        + [dma((pairs,))] * 4
        + [dma((pairs - 1,))] * 2
        + [dma((images - 1,))] * 2,
        compiler_params=pltpu.CompilerParams(
            collective_id=0, has_side_effects=True, vmem_limit_bytes=44 << 20
        ),
    )(*(pltpu.with_memory_space_constraint(array, pltpu.HBM) for array in (coeffs, triples, sketch)))


def hand_out_kernel(basis_ref, part_ref, basis_hbm, part_hbm, sems):
    step = basis_ref.shape[0] // PIECES
    copies = [pltpu.make_async_copy(part_ref, part_hbm, sems.at[PIECES])]
    for k in range(PIECES):
        here = pl.ds(k * step, step)
        copies.append(pltpu.make_async_copy(basis_ref.at[here], basis_hbm.at[here], sems.at[k]))
    for one in copies:
        one.start()
    for one in copies:
        one.wait()


def hand_out(basis, part):
    return pl.pallas_call(
        hand_out_kernel,
        in_specs=[VMEM] * 2,
        out_specs=[HBM] * 2,
        out_shape=[jax.ShapeDtypeStruct(basis.shape, basis.dtype), jax.ShapeDtypeStruct(part.shape, part.dtype)],
        scratch_shapes=[pltpu.SemaphoreType.DMA((PIECES + 1,))],
        compiler_params=pltpu.CompilerParams(vmem_limit_bytes=4 << 20),
    )(basis, part)


def on_device(coeffs, triples, sketch):
    rows_here = coeffs.shape[0]
    feats_here = triples.shape[1]
    img_count = lax.axis_size("img")
    feat_count = lax.axis_size("feat")
    total_rows = rows_here * img_count
    total_feats = feats_here * feat_count
    sketch_scale = (1.5 / total_feats) ** 0.5
    return hand_out(*factor_and_project(
        coeffs, triples, sketch, feat_count, img_count,
        sketch_scale * sketch_scale / total_rows, sketch_scale, total_rows**-0.5,
    ))


def solution(mesh):
    in_specs = (P("img", "feat"), P(None, "feat"), P("feat", None))
    out_specs = (P("img", None), P("img", "feat"))
    return jax.shard_map(
        on_device, mesh=mesh, in_specs=in_specs, out_specs=out_specs, check_vma=False
    )
```

```python
import functools

import jax
import jax.numpy as jnp
from jax import lax
from jax.experimental import pallas as pl
from jax.experimental.pallas import tpu as pltpu
from jax.sharding import PartitionSpec as P

CHUNKS = 8
AHEAD = (3, 1)
SUMMED = 5
EARLY = 2
SUB = 8
PANEL = 32
PIECES = 4
MESH = pl.DeviceIdType.MESH
VMEM = pl.BlockSpec(memory_space=pltpu.VMEM)
HBM = pl.BlockSpec(memory_space=pltpu.HBM)


def greet(groups):
    barrier = pltpu.get_barrier_semaphore()
    for axis, peers in groups:
        for peer in peers:
            pl.semaphore_signal(barrier, inc=1, device_id={axis: peer}, device_id_type=MESH)
    pl.semaphore_wait(barrier, sum(len(peers) for axis, peers in groups))


def peers_of(me, count):
    return [lax.rem(me + k, count) for k in range(1, count)]


def factor_panels(scale, after, gram, left, right, pivots, out_ref, width):
    size = gram.shape[0]
    rows = lax.broadcasted_iota(jnp.int32, (width, size), 0)
    lanes = lax.broadcasted_iota(jnp.int32, (width, size), 1)
    left[...] = gram * scale
    whole_rows = lax.broadcasted_iota(jnp.int32, (size, size), 0)
    whole_lanes = lax.broadcasted_iota(jnp.int32, (size, size), 1)
    right[...] = jnp.where(whole_rows == whole_lanes, 1.0, 0.0)

    def panel(p, carry):
        first = pl.multiple_of(p * width, width)
        here = pl.ds(first, width)
        block = left[here, :]
        twin = right[here, :]
        inverse = jnp.zeros((width, size), jnp.float32)
        for start in range(0, width, SUB):
            columns = [
                jnp.take_along_axis(block, jnp.full((width, size), first + start + j, jnp.int32), axis=1)
                for j in range(SUB)
            ]
            for j in range(SUB):
                at = start + j
                ratio = 1.0 / columns[j][at : at + 1, :]
                inverse = jnp.where(rows == at, ratio, inverse)
                if at + 1 < width:
                    factor = jnp.where(rows > at, columns[j] * ratio, 0.0)
                    for m in range(j + 1, SUB):
                        columns[m] = columns[m] - factor * columns[m][at : at + 1, :]
                    block = block - factor * block[at : at + 1, :]
                    twin = twin - factor * twin[at : at + 1, :]
        pivots[here, :] = inverse
        right[here, :] = twin

        @pl.when(p + 1 < size // width)
        def _():
            factor = jnp.where(lanes >= first + width, block * inverse, 0.0)
            across = (((0,), (0,)), ((), ()))
            exact = lax.Precision.HIGHEST
            left[...] -= lax.dot_general(factor, block, across, precision=exact, preferred_element_type=jnp.float32)
            right[...] -= lax.dot_general(factor, twin, across, precision=exact, preferred_element_type=jnp.float32)

        return carry

    lax.fori_loop(0, size // width, panel, 0)
    out_ref[...] = right[...] * (after * jnp.sqrt(pivots[...]))


def whole_kernel(
    count, images, width, scale, after, root, coeffs_hbm, triples_hbm, sketch_hbm, basis_ref, out_ref,
    triples_ref, sketch_ref, tile_ref, blocks, sel_ref, signs_ref, sum_ref, part_ref, slots, full_ref, gram_ref,
    inverse_ref, raw_ref, pair_gram, chip_gram, pair_staged, pair_raw, chip_staged, chip_raw, solved_ref, row_slots, left, right,
    pivots, own_sem, send_sem, recv_sem, to_sem, from_sem, out_sem, in_sem, gram_send, gram_recv, pair_send, pair_recv,
    chip_send, chip_recv, row_send, row_recv
):
    me = lax.axis_index("feat")
    spot = lax.axis_index("img")
    rows, part = coeffs_hbm.shape
    feats = triples_ref.shape[1]
    step = rows // CHUNKS
    half = count * part // 2
    tiles = feats // width
    spans = ((0, half), (half, half), (2 * half, 2 * half))

    def build(index):
        start, depth = spans[index]

        def one(j, carry):
            cols = pl.ds(pl.multiple_of(j * width, width), width)
            levels = lax.broadcasted_iota(jnp.int32, (depth, width), 0)
            chosen = triples_ref[index : index + 1, cols]
            sel_ref[start : start + depth, cols] = jnp.where(levels == chosen, 1.0, 0.0).astype(jnp.bfloat16)
            if index == 2:
                signs_ref[cols, :] = sketch_ref[cols, :].astype(jnp.float32).astype(jnp.bfloat16)
            return carry

        lax.fori_loop(0, tiles, one, 0)

    own = pltpu.make_async_copy(coeffs_hbm, blocks.at[me], own_sem.at[0])
    own.start()
    triples_copy = pltpu.make_async_copy(triples_hbm, triples_ref, own_sem.at[1])
    triples_copy.start()
    sketch_copy = pltpu.make_async_copy(sketch_hbm, sketch_ref, own_sem.at[2])
    sketch_copy.start()
    peers = peers_of(spot, images)
    greet((("feat", peers_of(me, count)), ("img", peers)))
    own.wait()
    triples_copy.wait()

    def copy(side, hop, chunk, source, target):
        span = blocks.at[source, pl.ds(pl.multiple_of(chunk * step, step), step)]
        return pltpu.make_async_remote_copy(
            src_ref=span,
            dst_ref=span,
            send_sem=send_sem.at[side, hop, chunk],
            recv_sem=recv_sem.at[side, hop, chunk],
            device_id={"feat": target},
            device_id_type=MESH,
        )

    owners = (count // 2 - 1, count // 2)
    piece = step // len(owners)

    def rows_of(chunk, o):
        return pl.ds(pl.multiple_of(chunk * step + o * piece, piece), piece)

    def reduce_copy(o, chunk, sender):
        return pltpu.make_async_remote_copy(
            src_ref=part_ref.at[rows_of(chunk, o)],
            dst_ref=slots.at[sender, chunk],
            send_sem=to_sem.at[o, chunk],
            recv_sem=from_sem.at[sender, chunk],
            device_id={"feat": owners[o]},
            device_id_type=MESH,
        )

    def spread_copy(o, chunk, target):
        span = full_ref.at[rows_of(chunk, o)]
        return pltpu.make_async_remote_copy(
            src_ref=span,
            dst_ref=span,
            send_sem=out_sem.at[target, chunk],
            recv_sem=in_sem.at[o, chunk],
            device_id={"feat": target},
            device_id_type=MESH,
        )

    def send_own(chunk, live):
        @pl.when(live & (me < count - 1))
        def _():
            copy(0, 0, chunk, me, me + 1).start()

        @pl.when(live & (me > 0))
        def _():
            copy(1, 0, chunk, me, me - 1).start()

    ahead = AHEAD[0] + (AHEAD[1] - AHEAD[0]) * lax.rem(spot, 2)
    for chunk in range(max(AHEAD)):
        send_own(chunk, chunk < ahead)

    def arrive(chunk):
        for o, owner in enumerate(owners):

            @pl.when(me != owner)
            def _():
                spread_copy(o, chunk, me).wait_recv()

    def add_up(start, stop):
        for chunk in range(start, stop):
            arrive(chunk)
        here = pl.ds(start * step, (stop - start) * step)
        value = full_ref[here, :]
        turned = value.T
        gram = jnp.dot(turned, value, preferred_element_type=jnp.float32)
        gram_ref[...] = gram if start == 0 else gram_ref[...] + gram

        def one_tile(j, unused):
            cols = pl.ds(pl.multiple_of(j * width, width), width)
            raw = jnp.dot(turned, tile_ref[here, cols], preferred_element_type=jnp.float32)
            raw_ref[:, cols] = raw if start == 0 else raw_ref[:, cols] + raw
            return unused

        lax.fori_loop(0, tiles, one_tile, 0)

    def one_round(turn, carry):
        for hop in range(count):
            chunk = turn - hop
            live = (chunk >= 0) & (chunk < CHUNKS)
            if hop > 0:

                @pl.when(live & (me >= hop))
                def _():
                    copy(0, hop - 1, chunk, me - hop, me - 1).wait_recv()

                @pl.when(live & (me + hop < count))
                def _():
                    copy(1, hop - 1, chunk, me + hop, me + 1).wait_recv()

            if 0 < hop < count - 1:

                @pl.when(live & (me >= hop) & (me < count - 1))
                def _():
                    copy(0, hop, chunk, me - hop, me + 1).start()

                @pl.when(live & (me + hop < count) & (me > 0))
                def _():
                    copy(1, hop, chunk, me + hop, me - 1).start()

        send_own(turn + ahead, (turn + ahead) < CHUNKS)
        for index in range(3):

            @pl.when(turn == min(index, count - 2))
            def _():
                if index == 2:
                    sketch_copy.wait()
                build(index)

        base = turn - (count - 1)
        for o, owner in enumerate(owners):

            @pl.when((base >= 1) & (base <= CHUNKS) & (me != owner))
            def _():
                reduce_copy(o, base - 1, me).start()

            @pl.when((base >= SUMMED) & (base <= CHUNKS + SUMMED - 1) & (me == owner))
            def _():
                mine = rows_of(base - SUMMED, o)
                total = part_ref[mine, :].astype(jnp.float32)
                for sender in range(count):
                    if sender != owner:
                        reduce_copy(o, base - SUMMED, sender).wait_recv()
                        total = total + slots[sender, base - SUMMED].astype(jnp.float32)
                full_ref[mine, :] = total.astype(jnp.bfloat16)
                for target in range(count):
                    if target != owner:
                        spread_copy(o, base - SUMMED, target).start()

        @pl.when((base >= 0) & (base < CHUNKS))
        def _():
            here = pl.ds(pl.multiple_of(base * step, step), step)
            sum_ref[...] = jnp.zeros(sum_ref.shape, jnp.float32)
            low = jnp.concatenate([blocks[s, here, :] for s in range(count // 2)], axis=1)
            high = jnp.concatenate([blocks[s, here, :] for s in range(count // 2, count)], axis=1)
            full = jnp.concatenate([low, high], axis=1)

            def one_tile(j, unused):
                cols = pl.ds(pl.multiple_of(j * width, width), width)
                first = jnp.dot(low, sel_ref[:half, cols], preferred_element_type=jnp.float32)
                second = jnp.dot(low, sel_ref[half : 2 * half, cols], preferred_element_type=jnp.float32)
                third = jnp.dot(full, sel_ref[2 * half :, cols], preferred_element_type=jnp.float32)
                tile = (first * second * third).astype(jnp.bfloat16)
                tile_ref[here, cols] = tile
                sum_ref[...] += jnp.dot(tile, signs_ref[cols, :], preferred_element_type=jnp.float32)
                return unused

            lax.fori_loop(0, tiles, one_tile, 0, unroll=4)
            part_ref[here, :] = sum_ref[...].astype(jnp.bfloat16)

        @pl.when(base == CHUNKS)
        def _():
            add_up(0, EARLY)

        return carry

    lax.fori_loop(0, CHUNKS + count - 1 + SUMMED, one_round, 0)
    add_up(EARLY, CHUNKS - 1)
    arrive(CHUNKS - 1)
    side = lax.rem(spot, 2)
    pairs = images // 2
    chips = [lax.rem(spot + 2 * k, images) for k in range(1, pairs)]
    span = feats // images
    rank_part = out_ref.shape[0]

    def columns(owner):
        return pl.ds(pl.multiple_of(owner * span, span), span)

    def remote(source, target, send, recv, device):
        return pltpu.make_async_remote_copy(
            src_ref=source, dst_ref=target, send_sem=send, recv_sem=recv, device_id={"img": device}, device_id_type=MESH
        )

    twin = spot + 1 - 2 * side
    mate = lax.div(spot, 2)
    order = [lax.rem(mate + k, pairs) for k in range(1, pairs + 1)]
    last = pl.ds((CHUNKS - 1) * step, step)
    value = full_ref[last, :]
    turned = value.T

    def raw_of(owner):
        return raw_ref[:, columns(owner)] + jnp.dot(
            turned, tile_ref[last, columns(owner)], preferred_element_type=jnp.float32
        )

    gram_ref[...] += jnp.dot(turned, value, preferred_element_type=jnp.float32)
    gram_pair = remote(gram_ref, pair_gram, gram_send.at[0], gram_recv.at[0], twin)
    gram_pair.start()
    pair_copies = []
    for k, m in enumerate(order):
        pair_staged[k] = raw_of(2 * m + 1 - side).astype(jnp.bfloat16)
        pair_copies.append(remote(pair_staged.at[k], pair_raw.at[k], pair_send.at[k], pair_recv.at[k], twin))
        pair_copies[-1].start()
    gram_pair.wait_recv()
    chip_gram[0] = gram_ref[...] + pair_gram[...]
    gram_copies = [
        remote(chip_gram.at[0], chip_gram.at[k + 1], gram_send.at[k + 1], gram_recv.at[k + 1], chip)
        for k, chip in enumerate(chips)
    ]
    for one in gram_copies:
        one.start()
    chip_copies = []
    for k, chip in enumerate(chips):
        both = raw_of(chip)
        pair_copies[k].wait_recv()
        chip_staged[k] = (both + pair_raw[k].astype(jnp.float32)).astype(jnp.bfloat16)
        chip_copies.append(remote(chip_staged.at[k], chip_raw.at[k], chip_send.at[k], chip_recv.at[k], chip))
        chip_copies[-1].start()
    mine = raw_of(spot)
    pair_copies[-1].wait_recv()
    mine = mine + pair_raw[pairs - 1].astype(jnp.float32)
    for one in gram_copies:
        one.wait_recv()
    total = jnp.zeros(gram_ref.shape, jnp.float32)
    for chip in range(pairs):
        total = total + chip_gram[lax.rem(lax.div(spot, 2) + pairs - chip, pairs)]
    factor_panels(scale, after, total, left, right, pivots, inverse_ref, min(PANEL, total.shape[0]))
    for k, one in enumerate(chip_copies):
        one.wait_recv()
        mine = mine + chip_raw[k].astype(jnp.float32)
    solved = jnp.dot(inverse_ref[...], mine, precision=lax.Precision.HIGHEST, preferred_element_type=jnp.float32) * root
    solved_ref[...] = solved.astype(jnp.bfloat16)

    def ranks(owner):
        return pl.ds(pl.multiple_of(owner * rank_part, rank_part), rank_part)

    row_copies = [
        remote(solved_ref.at[ranks(peer)], row_slots.at[k], row_send.at[k], row_recv.at[k], peer)
        for k, peer in enumerate(peers)
    ]
    for one in row_copies:
        one.start()
    high = inverse_ref[...].astype(jnp.bfloat16)
    rest = inverse_ref[...] - high.astype(jnp.float32)
    middle = rest.astype(jnp.bfloat16)
    low = (rest - middle.astype(jnp.float32)).astype(jnp.bfloat16)
    turn_back = (((1,), (1,)), ((), ()))

    def one_block(j, carry):
        here = pl.ds(pl.multiple_of(j * step, step), step)
        block = full_ref[here, :]
        made = [
            lax.dot_general(block, piece, turn_back, preferred_element_type=jnp.float32) for piece in (low, middle, high)
        ]
        basis_ref[here, :] = made[0] + made[1] + made[2]
        return carry

    lax.fori_loop(0, CHUNKS, one_block, 0)
    out_ref[:, columns(spot)] = solved_ref[ranks(spot), :].astype(jnp.float32)

    def drain(chunk, carry):
        for o, owner in enumerate(owners):

            @pl.when(me != owner)
            def _():
                reduce_copy(o, chunk, me).wait_send()

            @pl.when(me == owner)
            def _():
                for target in range(count):
                    if target != owner:
                        spread_copy(o, chunk, target).wait_send()

        for hop in range(count - 1):

            @pl.when((me >= hop) & (me < count - 1))
            def _():
                copy(0, hop, chunk, me - hop, me + 1).wait_send()

            @pl.when((me + hop < count) & (me > 0))
            def _():
                copy(1, hop, chunk, me + hop, me - 1).wait_send()

        return carry

    lax.fori_loop(0, CHUNKS, drain, 0)
    for k, one in enumerate(row_copies):
        one.wait_recv()
        out_ref[:, columns(lax.rem(spot + images - 1 - k, images))] = row_slots[k].astype(jnp.float32)
    for one in [gram_pair] + pair_copies + gram_copies + chip_copies + row_copies:
        one.wait_send()


def factor_and_project(coeffs, triples, sketch, count, images, scale, after, root):
    rows, part = coeffs.shape
    feats, rank = sketch.shape
    hops = max(count - 1, 1)
    step = rows // CHUNKS
    pairs = images // 2
    span = feats // images
    rank_part = rank // images
    square = pltpu.VMEM((rank, rank), jnp.float32)
    dma = pltpu.SemaphoreType.DMA
    return pl.pallas_call(
        functools.partial(whole_kernel, count, images, min(1024, feats), scale, after, root),
        in_specs=[HBM] * 3,
        out_specs=[VMEM] * 2,
        out_shape=[
            jax.ShapeDtypeStruct((rows, rank), jnp.float32),
            jax.ShapeDtypeStruct((rank_part, feats), jnp.float32),
        ],
        scratch_shapes=[
            pltpu.VMEM(triples.shape, jnp.int32),
            pltpu.VMEM((feats, rank), jnp.int32),
            pltpu.VMEM((rows, feats), jnp.bfloat16),
            pltpu.VMEM((count, rows, part), jnp.bfloat16),
            pltpu.VMEM((2 * count * part, feats), jnp.bfloat16),
            pltpu.VMEM((feats, rank), jnp.bfloat16),
            pltpu.VMEM((step, rank), jnp.float32),
            pltpu.VMEM((rows, rank), jnp.bfloat16),
            pltpu.VMEM((count, CHUNKS, step // 2, rank), jnp.bfloat16),
            pltpu.VMEM((rows, rank), jnp.bfloat16),
            square,
            square,
            pltpu.VMEM((rank, feats), jnp.float32),
            square,
            pltpu.VMEM((pairs, rank, rank), jnp.float32),
            pltpu.VMEM((pairs, rank, span), jnp.bfloat16),
            pltpu.VMEM((pairs, rank, span), jnp.bfloat16),
            pltpu.VMEM((pairs - 1, rank, span), jnp.bfloat16),
            pltpu.VMEM((pairs - 1, rank, span), jnp.bfloat16),
            pltpu.VMEM((rank, span), jnp.bfloat16),
            pltpu.VMEM((images - 1, rank_part, span), jnp.bfloat16),
            square,
            square,
            square,
            dma((3,)),
            dma((2, hops, CHUNKS)),
            dma((2, hops, CHUNKS)),
            dma((2, CHUNKS)),
            dma((count, CHUNKS)),
            dma((count, CHUNKS)),
            dma((2, CHUNKS)),
        ]
        + [dma((pairs,))] * 4
        + [dma((pairs - 1,))] * 2
        + [dma((images - 1,))] * 2,
        compiler_params=pltpu.CompilerParams(
            collective_id=0, has_side_effects=True, vmem_limit_bytes=44 << 20
        ),
    )(*(pltpu.with_memory_space_constraint(array, pltpu.HBM) for array in (coeffs, triples, sketch)))


def hand_out_kernel(basis_ref, part_ref, basis_hbm, part_hbm, sems):
    step = basis_ref.shape[0] // PIECES
    copies = [pltpu.make_async_copy(part_ref, part_hbm, sems.at[PIECES])]
    for k in range(PIECES):
        here = pl.ds(k * step, step)
        copies.append(pltpu.make_async_copy(basis_ref.at[here], basis_hbm.at[here], sems.at[k]))
    for one in copies:
        one.start()
    for one in copies:
        one.wait()


def hand_out(basis, part):
    return pl.pallas_call(
        hand_out_kernel,
        in_specs=[VMEM] * 2,
        out_specs=[HBM] * 2,
        out_shape=[jax.ShapeDtypeStruct(basis.shape, basis.dtype), jax.ShapeDtypeStruct(part.shape, part.dtype)],
        scratch_shapes=[pltpu.SemaphoreType.DMA((PIECES + 1,))],
        compiler_params=pltpu.CompilerParams(vmem_limit_bytes=4 << 20),
    )(basis, part)


def on_device(coeffs, triples, sketch):
    rows_here = coeffs.shape[0]
    feats_here = triples.shape[1]
    img_count = lax.axis_size("img")
    feat_count = lax.axis_size("feat")
    total_rows = rows_here * img_count
    total_feats = feats_here * feat_count
    sketch_scale = (1.5 / total_feats) ** 0.5
    return hand_out(*factor_and_project(
        coeffs, triples, sketch, feat_count, img_count,
        sketch_scale * sketch_scale / total_rows, sketch_scale, total_rows**-0.5,
    ))


def solution(mesh):
    in_specs = (P("img", "feat"), P(None, "feat"), P("feat", None))
    out_specs = (P("img", None), P("img", "feat"))
    return jax.shard_map(
        on_device, mesh=mesh, in_specs=in_specs, out_specs=out_specs, check_vma=False
    )
```
